256 devices in a mesh: sect: 4 (over x_lo, core), slab: 64 (over x_hi, y, z).
Axes of the slice: x: 4 (x_hi: 2, x_lo: 2; x = x_hi * 2 + x_lo), y: 4, z: 8, core: 2. Of those that a mesh axis runs over, the one named last changes fastest.
Arguments:
- density: float32 [512, 128, 128], P('slab', 'sect'), may hold values from 0.3 to 3
- velocity: float32 [3, 512, 128, 128], P(None, 'slab', 'sect'), may hold values from -4.8 to 4.8, as said below
- pressure: float32 [512, 128, 128], P('slab', 'sect'), may hold values from 0.3 to 3
- owners: int32 [128, 4, 1], P('sect'), may hold values from 0 to 63; in each aligned block of 128 rows (0 to 127, 128 to 255, ..., all dimensions but the last counted through in order) at most 4 rows name the same one
Outputs:
- new_state: float32 [5, 512, 128, 128], P(None, 'slab', 'sect')
- optical_depth: float32 [4, 64, 4, 512], P('sect', 'slab')
The draws below stay inside these ranges and needn't reach their ends.
Inputs may be any that keep to these rules, and one draw needn't show every extreme that they name: velocity components are real values within the range. `owners`: among the sightlines of one section (the aligned block of 128 rows) no index is named more than 4 times, a bound that some block reaches.
All inputs are finite; a program needn't handle non-finite values. Where the reference program divides by a largest or mean magnitude, that divisor is 1e-20 or more.
Results may differ from the reference program's by a relative error of at most 0.0001.
Values sent between devices are 32-bit elements; how exact they have to be, the bound alone decides.
A program may use at most 128 MiB of HBM per device.

```python
import math
import jax
import jax.numpy as jnp
import numpy as np
from jax import lax

CY = 32
NZ = 128
STRIDE = 32
BAND = 512
NX = 512
NY = 128
LINES = 4
MOST = 4
N_SECT = 4
N_SLAB = 64


def draw_velocity(key, part):
    position = jnp.arange(NX, dtype=jnp.float32) / (NX - 1)
    scaling = 0.4 + 0.8 * position
    values = jnp.clip(jax.random.normal(key, (3, NX, NY, NZ), jnp.float32), -4.0, 4.0)
    return values * scaling[None, :, None, None]


def block_levels(key, extent, cuts, least, high):
    factor_of = 1.0
    for dim, blocks in cuts:
        draws = jax.random.uniform(jax.random.fold_in(jax.random.fold_in(key, 6), dim), (blocks,), jnp.float32, least / len(cuts), high / len(cuts))
        factor_of = factor_of * jnp.repeat(jnp.exp(draws), extent[dim] // blocks).reshape((-1,) + (1,) * (len(extent) - 1 - dim))
    return factor_of


def deal_out(key, own, number, rows, amount, top, reach, skew):
    order = jax.random.permutation(key, amount)
    packed, usual = shares(amount, rows * top, reach, skew, True), shares(amount, rows * top, reach, skew, False)
    places = jnp.arange(amount)

    def named(sizes, turn):
        used = int((sizes > 0).sum())
        fixed = max(1, used // 4)
        passed = fixed + (places - fixed + turn * (used - fixed)) % max(1, amount - fixed)
        return jnp.zeros((amount,), jnp.int32).at[order[jnp.where(places < fixed, places, passed)]].set(jnp.asarray(sizes, jnp.int32))

    sizes = jnp.where(number % 4 == 0, named(packed, number // 4), named(usual, number - number // 4 - 1))
    mixed = jax.random.permutation(jax.random.fold_in(own, 3), amount)
    source_of, sink = mixed[0:amount // 2 * 2:2], mixed[1:amount // 2 * 2:2]
    room = jnp.minimum(sizes[source_of] - 1, reach - sizes[sink]) // 2
    room = jnp.where((source_of == order[0]) | (sink == order[0]) | (sizes[sink] == 0), 0, jnp.maximum(room, 0))
    passed = jax.random.randint(jax.random.fold_in(own, 4), (amount // 2,), 0, 1 << 20) % (room + 1)
    sizes = sizes.at[source_of].add(-passed).at[sink].add(passed)
    members = jnp.searchsorted(jnp.cumsum(sizes), jnp.arange(rows * top), side="right").astype(jnp.int32)
    grid = members.reshape(top, rows).T
    grid = grid[jax.random.permutation(jax.random.fold_in(own, 1), rows)]
    turn = jax.random.randint(jax.random.fold_in(own, 2), (rows, 1), 0, top)
    return jnp.take_along_axis(grid, (jnp.arange(top)[None, :] + turn) % top, axis=1)


def shares(count, total, bound, skew, full):
    portions = [(1 << 20) // math.isqrt(standing ** skew) + 1 for standing in range(1, count + 1)]
    largest = bound if full else min(bound, max(-(-total // count), total * portions[0] // sum(portions)))
    least = 1 if total - largest >= count - 1 else 0
    holding, surplus = [largest] + [least] * (count - 1), total - largest - least * (count - 1)
    while surplus > 0:
        candidates = [i for i in range(1, count) if holding[i] < largest] or [i for i in range(1, count) if holding[i] < bound]
        mass, budget = sum([portions[i] for i in candidates]), surplus
        for i in candidates:
            more = min(bound - holding[i], max(1, budget * portions[i] // mass), surplus)
            holding[i] = holding[i] + more
            surplus = surplus - more
    return np.array(holding)


def setup_inputs(seed: int = 0) -> dict:
    key_of = jax.random.split(jax.random.key(seed), 5)
    density = jnp.clip(jnp.exp(math.log(3.0) - 2.3025851 * jax.random.uniform(key_of[0], (NX, NY, NZ), jnp.float32) ** block_levels(key_of[0], (NX, NY, NZ), ((0, 64), (1, 4)), -0.2, 0.2)), 0.3, 3.0)
    velocity = draw_velocity(jax.random.fold_in(key_of[4], 71), 0)
    pressure = jnp.clip(jnp.exp(math.log(3.0) - 2.3025851 * jax.random.uniform(key_of[2], (NX, NY, NZ), jnp.float32) ** block_levels(key_of[2], (NX, NY, NZ), ((0, 64), (1, 4)), -0.2, 0.2)), 0.3, 3.0)
    owners_keys = jax.random.split(jax.random.fold_in(key_of[3], 1), NY * LINES // (CY * LINES))
    owners_turns = jax.random.permutation(jax.random.fold_in(key_of[3], 3), NY * LINES // (CY * LINES))
    owners = jax.vmap(lambda own, number: deal_out(jax.random.fold_in(key_of[3], 2), own, number, CY * LINES, N_SLAB, 1, MOST, 2))(owners_keys, owners_turns).reshape((NY, LINES, 1))
    return dict(density=density, velocity=velocity, pressure=pressure, owners=owners)


GAMMA = 5.0 / 3.0
COURANT = 0.15
TURBULENT = 0.25
NORMALISE = 0.5641895835477563

def primitives(current):
    density = current[0]
    velocity = current[1:4] / density
    pressure = (GAMMA - 1.0) * (current[4] - 0.5 * lax.optimization_barrier(jnp.sum(current[1:4] * velocity, axis=0)))
    return (density, velocity, pressure)

def conserved(density, velocity, pressure):
    momentum = density[None] * velocity
    energy = pressure / (GAMMA - 1.0) + 0.5 * lax.optimization_barrier(jnp.sum(momentum * velocity, axis=0))
    return jnp.concatenate([density[None], momentum, energy[None]], axis=0)

def physical_flux(current, velocity, pressure, axis_dim):
    moving = velocity[axis_dim]
    pieces = [current[axis_dim + 1]]
    for component in range(3):
        summand = current[component + 1] * moving
        if component == axis_dim:
            summand = summand + pressure
        pieces.append(summand)
    pieces.append((current[4] + pressure) * moving)
    return jnp.stack(pieces, axis=0)

def face_flux(left_state, right_state, axis_dim):
    left_density, left_velocity, left_pressure = primitives(left_state)
    right_density, right_velocity, right_pressure = primitives(right_state)
    left_speed = jnp.abs(left_velocity[axis_dim]) + jnp.sqrt(GAMMA * left_pressure / left_density)
    right_speed = jnp.abs(right_velocity[axis_dim]) + jnp.sqrt(GAMMA * right_pressure / right_density)
    signal_speed = jnp.maximum(left_speed, right_speed)
    average = 0.5 * (physical_flux(left_state, left_velocity, left_pressure, axis_dim) + physical_flux(right_state, right_velocity, right_pressure, axis_dim))
    return average - 0.5 * signal_speed[None] * (right_state - left_state)

def line_inputs(current):
    density, velocity, pressure = primitives(current)
    broadening = TURBULENT + pressure / density
    return jnp.stack([density, broadening, velocity[0]], axis=0)

def line_params(fields):
    width = BAND / 64.0 * jnp.sqrt(fields[1])
    amplitude = NORMALISE * jnp.square(fields[0]) * jnp.power(fields[1], -0.7) / width
    return jnp.stack([amplitude, 1.0 / width, BAND / 8.0 * fields[2]], axis=0)

def line_depth(params):
    half_band = BAND // 2

    def add_offset(position, running):
        offset = (position - half_band).astype(jnp.float32)
        summand = params[0] * jnp.exp(-jnp.square((offset - params[2]) * params[1]))
        return running + jnp.roll(summand, position - half_band, axis=1)
    return lax.fori_loop(0, BAND, add_offset, jnp.zeros(params.shape[1:], jnp.float32))

def reference(density, velocity, pressure, owners):
    current = conserved(density, velocity, pressure)
    sound_speed = jnp.sqrt(GAMMA * pressure / density)
    fastest = jnp.max(jnp.abs(velocity) + sound_speed[None])
    time_step = COURANT / fastest
    change = jnp.zeros_like(current)
    for axis_dim in range(3):
        face_term = face_flux(current, jnp.roll(current, -1, axis=axis_dim + 1), axis_dim)
        change = change + (face_term - jnp.roll(face_term, 1, axis=axis_dim + 1))
    new_state = current - time_step * change
    fields = line_inputs(new_state[:, :, :, ::STRIDE])
    params = line_params(fields)
    columns = jnp.transpose(params, (0, 2, 3, 1)).reshape(3, NY * LINES, NX)
    skewers = line_depth(columns)
    owner_rows = owners.reshape(N_SECT, CY * LINES)
    choose = (owner_rows[:, :, None] == jnp.arange(N_SLAB, dtype=jnp.int32)[None, None, :]).astype(jnp.int32)
    ranking = lax.optimization_barrier(jnp.sum((jnp.cumsum(choose, axis=1) - choose) * choose, axis=2))
    target = owner_rows * MOST + ranking
    sections = jnp.arange(N_SECT, dtype=jnp.int32)[:, None]
    placed = jnp.zeros((N_SECT, N_SLAB * MOST, NX), jnp.float32)
    placed = placed.at[sections, target].set(skewers.reshape(N_SECT, CY * LINES, NX))
    return (new_state, placed.reshape(N_SECT, N_SLAB, MOST, NX))
```

```python
import functools
import math

import jax
import jax.numpy as jnp
from jax import lax
from jax.experimental import pallas as pl
from jax.experimental.pallas import tpu as pltpu
from jax.sharding import PartitionSpec as P

MESH = pl.DeviceIdType.MESH
GAMMA = 5.0 / 3.0
COURANT = 0.15
TURBULENT = 0.25
NORMALISE = 0.5641895835477563
NSLAB = 64
NSECT = 4
NXL = 8
CY = 32
NZ = 128
MOST = 4
NX = 512
LOG2E = math.log2(math.e)
F32 = jnp.float32


def state(prim):
    r, v0, v1, v2, p = prim
    m0, m1, m2 = r * v0, r * v1, r * v2
    energy = 1.5 * p + 0.5 * (m0 * v0 + m1 * v1 + m2 * v2)
    return (r, m0, m1, m2, energy)


def sound(prim):
    return jnp.sqrt(GAMMA * (prim[4] / prim[0]))


def side(prim, w, c, d):
    moving, p = prim[1 + d], prim[4]
    flux = [w[1 + d], w[1] * moving, w[2] * moving, w[3] * moving, (w[4] + p) * moving]
    flux[1 + d] = flux[1 + d] + p
    return w, flux, jnp.abs(moving) + c


def face(left, right):
    (wl, fl, al), (wr, fr, ar) = left, right
    a = jnp.maximum(al, ar)
    return [(fl[k] + fr[k]) - a * (wr[k] - wl[k]) for k in range(5)]


def cell(prim, d):
    return side(prim, state(prim), sound(prim), d)


def iota(shape, dim):
    return lax.broadcasted_iota(jnp.int32, shape, dim)


def comm_kernel(den, vel, pre, own, w_out, d_out, r_out, U, hs, hr, ms, mr, cs, xs, oh, ps, in_sem, hs_sem, hr_sem, xs_sem, xr_sem,
                loc_sem, as_sem, ar_sem):
    me = lax.axis_index("slab")
    sect = lax.axis_index("sect")

    inner = (pl.ds(1, NXL), pl.ds(8, CY))
    copies = [
        pltpu.make_async_copy(den, U.at[(0,) + inner], in_sem.at[0]),
        pltpu.make_async_copy(vel, U.at[(pl.ds(1, 3),) + inner], in_sem.at[1]),
        pltpu.make_async_copy(pre, U.at[(4,) + inner], in_sem.at[2]),
    ]
    for c in copies:
        c.start()

    barrier = pltpu.get_barrier_semaphore()

    def greet(i, carry):
        pl.semaphore_signal(barrier, inc=1, device_id={"slab": lax.rem(me + i, NSLAB)}, device_id_type=MESH)
        return carry

    lax.fori_loop(1, NSLAB, greet, 0)
    for i in range(1, NSECT):
        pl.semaphore_signal(barrier, inc=1, device_id={"sect": lax.rem(sect + i, NSECT)}, device_id_type=MESH)

    row = jnp.concatenate([own[k].astype(F32) for k in range(4)], axis=1)
    across = jnp.broadcast_to(row, (128, 128))
    down = jnp.transpose(across)
    lane, sub = iota((128, 128), 1), iota((128, 128), 0)
    count = lambda i: lax.rem(i, 32) * 4 + i // 32
    earlier = jnp.where((across == down) & (count(sub) < count(lane)), 1.0, 0.0)
    rank = jnp.sum(earlier, axis=0, keepdims=True)
    target = row * MOST + rank
    slots = iota((NSLAB * MOST, 128), 0).astype(F32)
    oh[...] = jnp.where(slots == target, 1.0, 0.0).astype(jnp.bfloat16)

    for c in copies:
        c.wait()

    def local_max(x, best):
        for yb in range(4):
            prim = [U[f, x + 1, 8 + 8 * yb:16 + 8 * yb, :] for f in range(5)]
            top = jnp.maximum(jnp.maximum(jnp.abs(prim[1]), jnp.abs(prim[2])), jnp.abs(prim[3])) + sound(prim)
            best = jnp.maximum(best, top)
        return best

    best = lax.fori_loop(0, NXL, local_max, jnp.zeros((8, 128), F32))
    best = jnp.broadcast_to(jnp.max(best, keepdims=True), (8, 128))
    ms[...] = best
    for f in range(5):
        hs[0, f] = U[f, 1:9, 39, :]
        hs[1, f] = U[f, 1:9, 8, :]
    hs[0, 5] = best
    hs[1, 5] = best

    pl.semaphore_wait(barrier, NSLAB - 1 + NSECT - 1)

    def remote(src, dst, ssem, rsem, where):
        return pltpu.make_async_remote_copy(src_ref=src, dst_ref=dst, send_sem=ssem, recv_sem=rsem, device_id=where,
                                            device_id_type=MESH)

    near = [
        remote(hs.at[0], hr.at[0], hs_sem.at[0], hr_sem.at[0], {"sect": lax.rem(sect + 1, NSECT)}),
        remote(hs.at[1], hr.at[1], hs_sem.at[1], hr_sem.at[1], {"sect": lax.rem(sect + NSECT - 1, NSECT)}),
        remote(ms, mr, hs_sem.at[2], hr_sem.at[2], {"sect": lax.rem(sect + 2, NSECT)}),
    ]
    ends = [
        remote(U.at[:, 8, pl.ds(8, CY)], U.at[:, 0, pl.ds(8, CY)], xs_sem.at[0], xr_sem.at[0], {"slab": lax.rem(me + 1, NSLAB)}),
        remote(U.at[:, 1, pl.ds(8, CY)], U.at[:, 9, pl.ds(8, CY)], xs_sem.at[1], xr_sem.at[1],
               {"slab": lax.rem(me + NSLAB - 1, NSLAB)}),
    ]
    for c in near:
        c.start()
    for c in ends:
        c.start()

    wide = iota((CY, 128), 1)
    wide32 = lax.rem(wide, 32)
    for f in range(5):
        packed = jnp.ones((CY, 128), F32)
        for x in range(NXL):
            tile = U[f, x + 1, 8:40, :]
            for step in (-1, 0, 1):
                n = x + 8 * (step + 1)
                shift = (n - step) % 128
                packed = jnp.where(wide32 == n, pltpu.roll(tile, shift, 1) if shift else tile, packed)
        cs[f, 8:40, :] = packed

    for c in near:
        c.wait_recv()
    best = jnp.maximum(jnp.maximum(best, hr[0, 5]), jnp.maximum(hr[1, 5], mr[...]))
    l8, s8 = iota((8, 128), 1), iota((8, 128), 0)
    pick = lax.rem(l8, 32) == s8 + 8
    for f in range(5):
        for way, to in ((0, 7), (1, 40)):
            turned = pltpu.roll(hr[way, f], 8, 1, stride=1, stride_axis=0)
            cs[f, to:to + 1, :] = jnp.sum(jnp.where(pick, turned, 0.0), axis=0, keepdims=True)

    l8_32 = lax.rem(l8, 32)
    middle = (l8_32 >= 8) & (l8_32 < 16)
    for yb in range(4):
        here = [cs[f, 8 + 8 * yb:16 + 8 * yb, :] for f in range(5)]
        above = [cs[f, 9 + 8 * yb:17 + 8 * yb, :] for f in range(5)]
        below = [cs[f, 7 + 8 * yb:15 + 8 * yb, :] for f in range(5)]
        w, c = state(here), sound(here)
        nextz = [pltpu.roll(a, 120, 1) for a in here]
        fz = face(side(here, w, c, 2), cell(nextz, 2))
        mid = side(here, w, c, 1)
        fu, fd = face(mid, cell(above, 1)), face(cell(below, 1), mid)
        moved = [(fu[k] - fd[k]) + (fz[k] - pltpu.roll(fz[k], 8, 1)) for k in range(5)]
        items = [jnp.where(middle, a, 0.0) for a in list(here) + moved]
        groups = []
        for g in range(3):
            total = None
            for j, item in enumerate(items[4 * g:4 * g + 4]):
                shift = (8 * j - 8) % 128
                part = pltpu.roll(item, shift, 1) if shift else item
                total = part if total is None else total + part
            groups.append(total)
        for k in range(4):
            block = jnp.zeros((8, 128), F32)
            for g in range(3):
                shift = (32 * g - 32 * k) % 128
                part = pltpu.roll(groups[g], shift, 1) if shift else groups[g]
                block = jnp.where(l8 // 32 == g, part, block)
            xs[32 * k + 8 * yb:32 * k + 8 * yb + 8, :] = block

    lines = xs[...]
    hi = lines.astype(jnp.bfloat16)
    rest = lines - hi.astype(F32)
    mid = rest.astype(jnp.bfloat16)
    lo = (rest - mid.astype(F32)).astype(jnp.bfloat16)
    chosen = oh[...]
    dot = functools.partial(jnp.dot, preferred_element_type=F32)
    sent = dot(chosen, hi) + (dot(chosen, mid) + dot(chosen, lo))
    sent = jnp.where(iota((NSLAB * MOST, 128), 1) >= 80, jnp.broadcast_to(best[0:1, :], (NSLAB * MOST, 128)), sent)
    ps[...] = sent.reshape(NSLAB, MOST, 128)

    def deliver(i, carry):
        q = lax.rem(me + i, NSLAB)
        remote(ps.at[q], r_out.at[me], as_sem, ar_sem, {"slab": q}).start()
        return carry

    lax.fori_loop(1, NSLAB, deliver, 0)
    mine = pltpu.make_async_copy(ps.at[me], r_out.at[me], loc_sem)
    mine.start()

    for f in range(5):
        U[f, 1:9, 7, :] = hr[0, f]
        U[f, 1:9, 40, :] = hr[1, f]
    for c in ends:
        c.wait_recv()

    def dense(x, carry):
        for yb in range(4):
            lo, hi = 8 + 8 * yb, 16 + 8 * yb
            here = [U[f, x + 1, lo:hi, :] for f in range(5)]
            w, c = state(here), sound(here)
            fz = face(side(here, w, c, 2), cell([pltpu.roll(a, 127, 1) for a in here], 2))
            moved = [fz[k] - pltpu.roll(fz[k], 1, 1) for k in range(5)]
            for d, pair in ((1, ((1, 1), (1, -1))), (0, ((2, 0), (0, 0)))):
                (xu, yu), (xd, yd) = pair
                mid = side(here, w, c, d)
                fu = face(mid, cell([U[f, x + xu, lo + yu:hi + yu, :] for f in range(5)], d))
                fd = face(cell([U[f, x + xd, lo + yd:hi + yd, :] for f in range(5)], d), mid)
                moved = [moved[k] + (fu[k] - fd[k]) for k in range(5)]
            for k in range(5):
                w_out[k, x, lo - 8:hi - 8, :] = w[k]
                d_out[k, x, lo - 8:hi - 8, :] = moved[k]
        return carry

    lax.fori_loop(0, NXL, dense, 0)

    mine.wait()
    for c in near + ends:
        c.wait_send()
    most = pl.ds(0, NSLAB - 1)
    pltpu.make_async_copy(ps.at[most], ps.at[most], as_sem).wait()
    pltpu.make_async_copy(r_out.at[most], r_out.at[most], ar_sem).wait()


def final_kernel(w_ref, d_ref, r_ref, own, new_hbm, od, nb, table, sem):
    me = lax.axis_index("slab").astype(F32)
    arrived = r_ref[...]
    fastest = jnp.max(jnp.max(arrived, axis=0), axis=0, keepdims=True)[:, 96:97]
    half_dt = (0.5 * COURANT) / fastest
    hdt = jnp.broadcast_to(half_dt, (8, 128))

    def advance(x, carry):
        for k in range(5):
            for yb in range(4):
                at = (k, x, slice(8 * yb, 8 * yb + 8))
                nb[at] = w_ref[at] - hdt * d_ref[at]
        return carry

    lax.fori_loop(0, NXL, advance, 0)
    out = pltpu.make_async_copy(nb, new_hbm, sem)
    out.start()

    l8, s8 = iota((8, 128), 1), iota((8, 128), 0)
    for u in range(64):
        o = l8 - s8 + 8 * u
        o = jnp.where(o >= NX // 2, o - NX, o)
        table[u] = o.astype(F32)

    turned = jnp.transpose(arrived.reshape(NSLAB * MOST, 128))
    fields = [turned[8 * f:8 * f + 8, :] for f in range(10)]
    here, moved = fields[:5], fields[5:]
    s2 = iota((8, NSLAB * MOST), 0)

    def after(a):
        a = pltpu.roll(a, 7, 0)
        return jnp.where(s2 < 7, a, pltpu.roll(a, NSLAB * MOST - 4, 1))

    def before(a):
        a = pltpu.roll(a, 1, 0)
        return jnp.where(s2 > 0, a, pltpu.roll(a, 4, 1))

    w = state(here)
    fx = face(side(here, w, sound(here), 0), cell([after(a) for a in here], 0))
    hdt2 = jnp.broadcast_to(half_dt, (8, NSLAB * MOST))
    new = [w[k] - hdt2 * (moved[k] + (fx[k] - before(fx[k]))) for k in range(5)]
    r = new[0]
    v = [new[1 + k] / r for k in range(3)]
    p = (GAMMA - 1.0) * (new[4] - 0.5 * (new[1] * v[0] + new[2] * v[1] + new[3] * v[2]))
    broad = TURBULENT + p / r
    inverse = math.sqrt(LOG2E) / (8.0 * jnp.sqrt(broad))
    moved_by = (64.0 * v[0]) * inverse
    level = jnp.log2((NORMALISE / 8.0) * (r * r)) - 1.2 * jnp.log2(broad)

    def some(pb, carry):
        inv, mov, lev, sums = carry
        sums = list(sums)
        for pp in range(8):
            tiles = [table[lax.rem(16 * it + 128 - 8 * pb - pp, 64)] for it in range(4)]
            for t in range(4):
                n = 4 * pp + t
                i_b = jnp.broadcast_to(inv[:, n:n + 1], (8, 128))
                m_b = jnp.broadcast_to(mov[:, n:n + 1], (8, 128))
                l_b = jnp.broadcast_to(lev[:, n:n + 1], (8, 128))
                for it in range(4):
                    z = tiles[it] * i_b - m_b
                    sums[4 * t + it] = sums[4 * t + it] + jnp.exp2(l_b - z * z)
        turn = lambda a: pltpu.roll(a, NSLAB * MOST - 32, 1)
        return turn(inv), turn(mov), turn(lev), tuple(sums)

    zero = jnp.zeros((8, 128), F32)
    sums = lax.fori_loop(0, 8, some, (inverse, moved_by, level, (zero,) * 16))[3]
    row = jnp.concatenate([own[k].astype(F32) for k in range(4)], axis=1)
    held = jnp.sum(jnp.where(row == me, 1.0, 0.0), axis=1, keepdims=True)
    for t in range(4):
        line = jnp.concatenate([jnp.sum(sums[4 * t + it], axis=0, keepdims=True) for it in range(4)], axis=1)
        od[0, 0, t:t + 1, :] = jnp.where(held > t, line, 0.0)
    out.wait()


def body(density, velocity, pressure, owners):
    own = jnp.transpose(owners, (1, 2, 0))
    vmem = pl.BlockSpec(memory_space=pltpu.VMEM)
    anyspace = pl.BlockSpec(memory_space=pl.ANY)
    dense = jax.ShapeDtypeStruct((5, NXL, CY, NZ), F32)
    arrived = jax.ShapeDtypeStruct((NSLAB, MOST, 128), F32)
    dma = pltpu.SemaphoreType.DMA
    w, d, r = pl.pallas_call(
        comm_kernel,
        out_shape=(dense, dense, arrived),
        in_specs=[anyspace, anyspace, anyspace, vmem],
        out_specs=(vmem, vmem, vmem),
        scratch_shapes=[
            pltpu.VMEM((5, NXL + 2, CY + 16, NZ), F32),
            pltpu.VMEM((2, 6, 8, 128), F32),
            pltpu.VMEM((2, 6, 8, 128), F32),
            pltpu.VMEM((8, 128), F32),
            pltpu.VMEM((8, 128), F32),
            pltpu.VMEM((5, CY + 16, 128), F32),
            pltpu.VMEM((128, 128), F32),
            pltpu.VMEM((NSLAB * MOST, 128), jnp.bfloat16),
            pltpu.VMEM((NSLAB, MOST, 128), F32),
            dma((3,)), dma((3,)), dma((3,)), dma((2,)), dma((2,)), dma, dma, dma,
        ],
        compiler_params=pltpu.CompilerParams(collective_id=0, has_side_effects=True, vmem_limit_bytes=24 << 20),
        name="exchange",
    )(density, velocity, pressure, own)
    return tuple(pl.pallas_call(
        final_kernel,
        out_shape=(dense, jax.ShapeDtypeStruct((1, 1, MOST, NX), F32)),
        in_specs=[vmem] * 4,
        out_specs=(anyspace, vmem),
        scratch_shapes=[pltpu.VMEM((5, NXL, CY, NZ), F32), pltpu.VMEM((64, 8, 128), F32), dma],
        compiler_params=pltpu.CompilerParams(vmem_limit_bytes=24 << 20),
        name="finish",
    )(w, d, r, own))


def solution(mesh):
    placed = (P("slab", "sect", None), P(None, "slab", "sect", None), P("slab", "sect", None), P("sect", None, None))
    return jax.shard_map(body, mesh=mesh, in_specs=placed, out_specs=(P(None, "slab", "sect", None), P("sect", "slab", None, None)),
                         check_vma=False)
```

```python
import functools
import math

import jax
import jax.numpy as jnp
from jax import lax
from jax.experimental import pallas as pl
from jax.experimental.pallas import tpu as pltpu
from jax.sharding import PartitionSpec as P

MESH = pl.DeviceIdType.MESH
GAMMA = 5.0 / 3.0
COURANT = 0.15
TURBULENT = 0.25
NORMALISE = 0.5641895835477563
NSLAB = 64
NSECT = 4
NXL = 8
CY = 32
NZ = 128
MOST = 4
NX = 512
F32 = jnp.float32
LOG2E = math.log2(math.e)
RINGS = ((1, 2), (1, 1), (1, 3), (0, 2), (1, 0), (0, 1), (0, 3))


def state(prim):
    r, v0, v1, v2, p = prim
    m0, m1, m2 = r * v0, r * v1, r * v2
    energy = 1.5 * p + 0.5 * (m0 * v0 + m1 * v1 + m2 * v2)
    return (r, m0, m1, m2, energy)


def sound(prim):
    return jnp.sqrt(GAMMA * (prim[4] / prim[0]))


def side(prim, w, c, d):
    moving, p = prim[1 + d], prim[4]
    flux = [w[1 + d], w[1] * moving, w[2] * moving, w[3] * moving, (w[4] + p) * moving]
    flux[1 + d] = flux[1 + d] + p
    return w, flux, jnp.abs(moving) + c


def face(left, right):
    (wl, fl, al), (wr, fr, ar) = left, right
    a = jnp.maximum(al, ar)
    return [(fl[k] + fr[k]) - a * (wr[k] - wl[k]) for k in range(5)]


def cell(prim, d):
    return side(prim, state(prim), sound(prim), d)


def iota(shape, dim):
    return lax.broadcasted_iota(jnp.int32, shape, dim)


def comm_kernel(den, vel, pre, own_hbm, w_out, d_out, r_out, table, U, hs, hr, cm, cr, ms, mr, cs, xs, oh, ps, own, in_sem, hs_sem,
                hr_sem, xs_sem, xr_sem, loc_sem, as_sem, ar_sem, back, go):
    me = lax.axis_index("slab")
    sect = lax.axis_index("sect")
    far, row_y, row_z = me // 32, lax.rem(me // 8, 4), lax.rem(me, 8)
    low, high = row_z < 4, row_z >= 4

    owned = pltpu.make_async_copy(own_hbm, own, in_sem.at[3])
    inner = (pl.ds(1, NXL), pl.ds(8, CY))
    copies = [
        pltpu.make_async_copy(den, U.at[(0,) + inner], in_sem.at[0]),
        pltpu.make_async_copy(vel, U.at[(pl.ds(1, 3),) + inner], in_sem.at[1]),
        pltpu.make_async_copy(pre, U.at[(4,) + inner], in_sem.at[2]),
    ]
    for c in copies:
        c.start()
    owned.start()

    def slab_of(step_x, step_y, z):
        return lax.rem(far + step_x, 2) * 32 + lax.rem(row_y + step_y, 4) * 8 + z

    barrier = pltpu.get_barrier_semaphore()
    for i in range(1, NSECT):
        pl.semaphore_signal(barrier, inc=1, device_id={"sect": lax.rem(sect + i, NSECT)}, device_id_type=MESH)

    def tell(sem, q):
        pl.semaphore_signal(sem, inc=1, device_id={"slab": q}, device_id_type=MESH)

    @pl.when(low)
    def _():
        for i in range(1, 4):
            tell(barrier, slab_of(0, 0, lax.rem(row_z + i, 4)))
        for i in range(4):
            tell(barrier, slab_of(0, 0, 4 + i))
        for a, b in RINGS:
            for z in range(8):
                tell(barrier, slab_of(a, b, z))

    @pl.when(high)
    def _():
        pl.semaphore_wait(barrier, 35)
        for a, b in ((0, 0),) + RINGS:
            for z in range(4):
                tell(back, slab_of(a, b, z))

    owned.wait()
    row = jnp.concatenate([own[k].astype(F32) for k in range(4)], axis=1)
    across = jnp.broadcast_to(row, (128, 128))
    down = jnp.transpose(across)
    lane, sub = iota((128, 128), 1), iota((128, 128), 0)
    count = lambda i: lax.rem(i, 32) * 4 + i // 32
    earlier = jnp.where((across == down) & (count(sub) < count(lane)), 1.0, 0.0)
    rank = jnp.sum(earlier, axis=0, keepdims=True)
    target = row * MOST + rank
    slots = iota((NSLAB * MOST, 128), 0).astype(F32)
    oh[...] = jnp.where(slots == target, 1.0, 0.0).astype(jnp.bfloat16)

    for c in copies:
        c.wait()

    l8, s8 = iota((8, 128), 1), iota((8, 128), 0)
    pick = lax.rem(l8, 32) == s8 + 8
    for f in range(5):
        for way, y in ((0, 39), (1, 8)):
            edge = U[f, 1:9, y, :]
            hs[way, f] = edge
            turned = pltpu.roll(edge, 8, 1, stride=1, stride_axis=0)
            cm[way, f:f + 1, :] = jnp.sum(jnp.where(pick, turned, 0.0), axis=0, keepdims=True)

    def local_max(x, best):
        for yb in range(4):
            prim = [U[f, x + 1, 8 + 8 * yb:16 + 8 * yb, :] for f in range(5)]
            top = jnp.maximum(jnp.maximum(jnp.abs(prim[1]), jnp.abs(prim[2])), jnp.abs(prim[3])) + sound(prim)
            best = jnp.maximum(best, top)
        return best

    best = lax.fori_loop(0, NXL, local_max, jnp.zeros((8, 128), F32))
    best = jnp.broadcast_to(jnp.max(best, keepdims=True), (8, 128))
    ms[...] = best
    for way in range(2):
        cm[way, 5:8, :] = best[5:8, :]

    @pl.when(low)
    def _():
        pl.semaphore_wait(barrier, 34)

    def remote(src, dst, ssem, rsem, where):
        return pltpu.make_async_remote_copy(src_ref=src, dst_ref=dst, send_sem=ssem, recv_sem=rsem, device_id=where,
                                            device_id_type=MESH)

    above_me, below_me = {"sect": lax.rem(sect + 1, NSECT)}, {"sect": lax.rem(sect + NSECT - 1, NSECT)}
    near = [
        remote(cm.at[0], cr.at[0], hs_sem.at[0], hr_sem.at[0], above_me),
        remote(cm.at[1], cr.at[1], hs_sem.at[1], hr_sem.at[1], below_me),
        remote(ms, mr, hs_sem.at[2], hr_sem.at[2], {"sect": lax.rem(sect + 2, NSECT)}),
    ]
    sides = [
        remote(hs.at[0], hr.at[0], hs_sem.at[3], hr_sem.at[3], above_me),
        remote(hs.at[1], hr.at[1], hs_sem.at[4], hr_sem.at[4], below_me),
    ]
    after, before = lax.rem(me + 1, NSLAB), lax.rem(me + NSLAB - 1, NSLAB)
    ends = [
        remote(U.at[:, 8, pl.ds(8, CY)], U.at[:, 0, pl.ds(8, CY)], xs_sem.at[0], xr_sem.at[0], {"slab": after}),
        remote(U.at[:, 1, pl.ds(8, CY)], U.at[:, 9, pl.ds(8, CY)], xs_sem.at[1], xr_sem.at[1], {"slab": before}),
    ]
    for c in near + sides:
        c.start()

    @pl.when((row_z < 3) | (row_z == 7))
    def _():
        ends[0].start()

    @pl.when((row_z > 0) & (row_z < 5))
    def _():
        ends[1].start()

    wide = iota((CY, 128), 1)
    wide32 = lax.rem(wide, 32)
    for f in range(5):
        packed = jnp.ones((CY, 128), F32)
        for x in range(NXL):
            tile = U[f, x + 1, 8:40, :]
            for step in (-1, 0, 1):
                n = x + 8 * (step + 1)
                shift = (n - step) % 128
                packed = jnp.where(wide32 == n, pltpu.roll(tile, shift, 1) if shift else tile, packed)
        cs[f, 8:40, :] = packed

    for c in near:
        c.wait_recv()
    best = jnp.maximum(jnp.maximum(best[5:6, :], cr[0, 5:6, :]), jnp.maximum(cr[1, 5:6, :], mr[5:6, :]))
    for f in range(5):
        cs[f, 7:8, :] = cr[0, f:f + 1, :]
        cs[f, 40:41, :] = cr[1, f:f + 1, :]

    l8_32 = lax.rem(l8, 32)
    middle = (l8_32 >= 8) & (l8_32 < 16)
    for yb in range(4):
        here = [cs[f, 8 + 8 * yb:16 + 8 * yb, :] for f in range(5)]
        above = [cs[f, 9 + 8 * yb:17 + 8 * yb, :] for f in range(5)]
        below = [cs[f, 7 + 8 * yb:15 + 8 * yb, :] for f in range(5)]
        w, c = state(here), sound(here)
        nextz = [pltpu.roll(a, 120, 1) for a in here]
        fz = face(side(here, w, c, 2), cell(nextz, 2))
        mid = side(here, w, c, 1)
        fu, fd = face(mid, cell(above, 1)), face(cell(below, 1), mid)
        moved = [(fu[k] - fd[k]) + (fz[k] - pltpu.roll(fz[k], 8, 1)) for k in range(5)]
        items = [jnp.where(middle, a, 0.0) for a in list(here) + moved]
        groups = []
        for g in range(3):
            total = None
            for j, item in enumerate(items[4 * g:4 * g + 4]):
                shift = (8 * j - 8) % 128
                part = pltpu.roll(item, shift, 1) if shift else item
                total = part if total is None else total + part
            groups.append(total)
        for k in range(4):
            block = jnp.zeros((8, 128), F32)
            for g in range(3):
                shift = (32 * g - 32 * k) % 128
                part = pltpu.roll(groups[g], shift, 1) if shift else groups[g]
                block = jnp.where(l8 // 32 == g, part, block)
            xs[32 * k + 8 * yb:32 * k + 8 * yb + 8, :] = block

    lines = xs[...]
    hi = lines.astype(jnp.bfloat16)
    rest = lines - hi.astype(F32)
    mid = rest.astype(jnp.bfloat16)
    lo = (rest - mid.astype(F32)).astype(jnp.bfloat16)
    chosen = oh[...]
    dot = functools.partial(jnp.dot, preferred_element_type=F32)
    sent = dot(chosen, hi) + (dot(chosen, mid) + dot(chosen, lo))
    sent = jnp.where(iota((NSLAB * MOST, 128), 1) >= 80, jnp.broadcast_to(best, (NSLAB * MOST, 128)), sent)
    ps[...] = sent.reshape(NSLAB, MOST, 128)

    def deliver(q):
        remote(ps.at[q], r_out.at[me], as_sem, ar_sem, {"slab": q}).start()

    def deliver_half(base):
        for a, b in RINGS:
            for z in range(4):
                deliver(slab_of(a, b, base + z))

    def deliver_own_ring(base):
        for i in range(1, 4):
            deliver(slab_of(0, 0, base + lax.rem(row_z + i, 4)))

    def deliver_other_ring(base):
        for z in range(4):
            deliver(slab_of(0, 0, base + z))

    @pl.when(low)
    def _():
        deliver_half(0)
        deliver_own_ring(0)

        pl.semaphore_wait(back, NSLAB // 2)

        @pl.when(row_z == 3)
        def _():
            tell(go, slab_of(0, 0, 4))
            tell(go, slab_of(0, 0, 5))
            ends[0].start()

        @pl.when(row_z == 0)
        def _():
            tell(go, slab_of(0, 0, 6))
            tell(go, slab_of(0, 0, 7))
            ends[1].start()

        deliver_half(4)
        deliver_other_ring(4)

    @pl.when(high)
    def _():
        deliver_half(0)
        deliver_other_ring(0)

        pl.semaphore_wait(go, 1)

        @pl.when(row_z < 7)
        def _():
            ends[0].start()

        @pl.when(row_z > 4)
        def _():
            ends[1].start()

        deliver_half(4)
        deliver_own_ring(4)

    mine = pltpu.make_async_copy(ps.at[me], r_out.at[me], loc_sem)
    mine.start()

    for u in range(65):
        o = s8 + (8 * u - 8) - 8 * (l8 // 4)
        o = jnp.where(o >= NX // 2, o - NX, o)
        table[8 * u:8 * u + 8, :] = o.astype(F32)

    for c in sides:
        c.wait_recv()
    for f in range(5):
        U[f, 1:9, 7, :] = hr[0, f]
        U[f, 1:9, 40, :] = hr[1, f]

    def dense(x, carry):
        for yb in range(4):
            lo, hi = 8 + 8 * yb, 16 + 8 * yb
            here = [U[f, x + 1, lo:hi, :] for f in range(5)]
            w, c = state(here), sound(here)
            fz = face(side(here, w, c, 2), cell([pltpu.roll(a, 127, 1) for a in here], 2))
            moved = [fz[k] - pltpu.roll(fz[k], 1, 1) for k in range(5)]
            for d, pair in ((1, ((1, 1), (1, -1))), (0, ((2, 0), (0, 0)))):
                (xu, yu), (xd, yd) = pair
                mid = side(here, w, c, d)
                fu = face(mid, cell([U[f, x + xu, lo + yu:hi + yu, :] for f in range(5)], d))
                fd = face(cell([U[f, x + xd, lo + yd:hi + yd, :] for f in range(5)], d), mid)
                moved = [moved[k] + (fu[k] - fd[k]) for k in range(5)]
            for k in range(5):
                w_out[k, x, lo - 8:hi - 8, :] = w[k]
                d_out[k, x, lo - 8:hi - 8, :] = moved[k]
        return carry

    lax.fori_loop(1, NXL - 1, dense, 0)
    for c in ends:
        c.wait_recv()
    lax.fori_loop(0, 2, lambda i, carry: dense((NXL - 1) * i, carry), 0)

    mine.wait()
    for c in near + sides + ends:
        c.wait_send()
    most = pl.ds(0, NSLAB - 1)
    pltpu.make_async_copy(ps.at[most], ps.at[most], as_sem).wait()
    pltpu.make_async_copy(r_out.at[most], r_out.at[most], ar_sem).wait()


def final_kernel(w_ref, d_ref, r_ref, table, own_hbm, new_hbm, od, nb, pb, acc, own, sem, own_sem):
    me = lax.axis_index("slab").astype(F32)
    owned = pltpu.make_async_copy(own_hbm, own, own_sem)
    owned.start()
    arrived = r_ref[...]
    fastest = jnp.max(jnp.max(arrived, axis=0), axis=0, keepdims=True)[:, 96:97]
    half_dt = (0.5 * COURANT) / fastest
    hdt = jnp.broadcast_to(half_dt, (8, 128))

    def advance(x, carry):
        for k in range(5):
            for yb in range(4):
                at = (k, x, slice(8 * yb, 8 * yb + 8))
                nb[at] = w_ref[at] - hdt * d_ref[at]
        return carry

    lax.fori_loop(0, NXL, advance, 0)
    out = pltpu.make_async_copy(nb, new_hbm, sem)
    out.start()

    turned = jnp.transpose(arrived.reshape(NSLAB * MOST, 128))
    fields = [turned[8 * f:8 * f + 8, :] for f in range(10)]
    here, moved = fields[:5], fields[5:]
    s2 = iota((8, NSLAB * MOST), 0)

    def after(a):
        a = pltpu.roll(a, 7, 0)
        return jnp.where(s2 < 7, a, pltpu.roll(a, NSLAB * MOST - 4, 1))

    def before(a):
        a = pltpu.roll(a, 1, 0)
        return jnp.where(s2 > 0, a, pltpu.roll(a, 4, 1))

    w = state(here)
    fx = face(side(here, w, sound(here), 0), cell([after(a) for a in here], 0))
    hdt2 = jnp.broadcast_to(half_dt, (8, NSLAB * MOST))
    new = [w[k] - hdt2 * (moved[k] + (fx[k] - before(fx[k]))) for k in range(5)]
    r = new[0]
    v = [new[1 + k] / r for k in range(3)]
    p = (GAMMA - 1.0) * (new[4] - 0.5 * (new[1] * v[0] + new[2] * v[1] + new[3] * v[2]))
    broad = TURBULENT + p / r
    inverse = math.sqrt(LOG2E) / (8.0 * jnp.sqrt(broad))
    moved_by = (64.0 * v[0]) * inverse
    level = jnp.log2((NORMALISE / 8.0) * (r * r)) - 1.2 * jnp.log2(broad)
    for n, param in enumerate((inverse, moved_by, level)):
        for h in range(2):
            for x in range(8):
                pb[n, 8 * h + x] = jnp.broadcast_to(param[x:x + 1, 128 * h:128 * h + 128], (8, 128))

    def pixels(block, carry):
        sums = [None] * 4
        for h in range(2):
            for x in range(8):
                inv, mov, lev = (pb[n, 8 * h + x] for n in range(3))
                for j in range(4):
                    u = lax.rem(4 * block + (j + 32 * h), 64)
                    o = table[pl.ds(8 * u + (8 - x), 8), :]
                    z = o * inv - mov
                    part = jnp.exp2(lev - z * z)
                    sums[j] = part if sums[j] is None else sums[j] + part
        for j in range(4):
            acc[pl.ds(pl.multiple_of(32 * block + 8 * j, 8), 8), :] = sums[j]
        return carry

    lax.fori_loop(0, 16, pixels, 0)
    depth = jnp.transpose(acc[...])
    both = depth[0:8, :]
    for n in range(1, 16):
        both = both + depth[8 * n:8 * n + 8, :]
    owned.wait()
    row = jnp.concatenate([own[k].astype(F32) for k in range(4)], axis=1)
    held = jnp.sum(jnp.where(row == me, 1.0, 0.0), axis=1, keepdims=True)
    valid = iota((4, NX), 0).astype(F32) < held
    od[0, 0] = jnp.where(valid, both[0:4, :] + both[4:8, :], 0.0)
    out.wait()


def body(density, velocity, pressure, owners):
    own = jnp.transpose(owners, (1, 2, 0))
    density, velocity, pressure, own = (pltpu.with_memory_space_constraint(a, pltpu.HBM) for a in (density, velocity, pressure, own))
    vmem = pl.BlockSpec(memory_space=pltpu.VMEM)
    hbm = pl.BlockSpec(memory_space=pltpu.HBM)
    dense = jax.ShapeDtypeStruct((5, NXL, CY, NZ), F32)
    arrived = jax.ShapeDtypeStruct((NSLAB, MOST, 128), F32)
    offsets = jax.ShapeDtypeStruct((NX + 8, 128), F32)
    dma, regular = pltpu.SemaphoreType.DMA, pltpu.SemaphoreType.REGULAR
    w, d, r, table = pl.pallas_call(
        comm_kernel,
        out_shape=(dense, dense, arrived, offsets),
        in_specs=[hbm, hbm, hbm, hbm],
        out_specs=(vmem, vmem, vmem, vmem),
        scratch_shapes=[
            pltpu.VMEM((5, NXL + 2, CY + 16, NZ), F32),
            pltpu.VMEM((2, 5, 8, 128), F32),
            pltpu.VMEM((2, 5, 8, 128), F32),
            pltpu.VMEM((2, 8, 128), F32),
            pltpu.VMEM((2, 8, 128), F32),
            pltpu.VMEM((8, 128), F32),
            pltpu.VMEM((8, 128), F32),
            pltpu.VMEM((5, CY + 16, 128), F32),
            pltpu.VMEM((128, 128), F32),
            pltpu.VMEM((NSLAB * MOST, 128), jnp.bfloat16),
            pltpu.VMEM((NSLAB, MOST, 128), F32),
            pltpu.VMEM((4, 1, CY), jnp.int32),
            dma((4,)), dma((5,)), dma((5,)), dma((2,)), dma((2,)), dma, dma, dma, regular, regular,
        ],
        compiler_params=pltpu.CompilerParams(collective_id=0, has_side_effects=True, vmem_limit_bytes=24 << 20),
        name="exchange",
    )(density, velocity, pressure, own)
    return tuple(pl.pallas_call(
        final_kernel,
        out_shape=(dense, jax.ShapeDtypeStruct((1, 1, MOST, NX), F32)),
        in_specs=[vmem, vmem, vmem, vmem, hbm],
        out_specs=(hbm, vmem),
        scratch_shapes=[
            pltpu.VMEM((5, NXL, CY, NZ), F32),
            pltpu.VMEM((3, 16, 8, 128), F32),
            pltpu.VMEM((NX, 128), F32),
            pltpu.VMEM((4, 1, CY), jnp.int32),
            dma, dma,
        ],
        compiler_params=pltpu.CompilerParams(vmem_limit_bytes=24 << 20),
        name="finish",
    )(w, d, r, table, own))


def solution(mesh):
    placed = (P("slab", "sect", None), P(None, "slab", "sect", None), P("slab", "sect", None), P("sect", None, None))
    return jax.shard_map(body, mesh=mesh, in_specs=placed, out_specs=(P(None, "slab", "sect", None), P("sect", "slab", None, None)),
                         check_vma=False)
```

```python
import functools
import math

import jax
import jax.numpy as jnp
from jax import lax
from jax.experimental import pallas as pl
from jax.experimental.pallas import tpu as pltpu
from jax.sharding import PartitionSpec as P

MESH = pl.DeviceIdType.MESH
GAMMA = 5.0 / 3.0
COURANT = 0.15
TURBULENT = 0.25
NORMALISE = 0.5641895835477563
NSLAB = 64
NSECT = 4
NXL = 8
CY = 32
NZ = 128
MOST = 4
NX = 512
F32 = jnp.float32
LOG2E = math.log2(math.e)
RINGS = ((1, 2), (1, 1), (1, 3), (0, 2), (1, 0), (0, 1), (0, 3))


def state(prim):
    r, v0, v1, v2, p = prim
    m0, m1, m2 = r * v0, r * v1, r * v2
    energy = 1.5 * p + 0.5 * (m0 * v0 + m1 * v1 + m2 * v2)
    return (r, m0, m1, m2, energy)


def sound(prim):
    return jnp.sqrt(GAMMA * (prim[4] / prim[0]))


def side(prim, w, c, d):
    moving, p = prim[1 + d], prim[4]
    flux = [w[1 + d], w[1] * moving, w[2] * moving, w[3] * moving, (w[4] + p) * moving]
    flux[1 + d] = flux[1 + d] + p
    return w, flux, jnp.abs(moving) + c


def face(left, right):
    (wl, fl, al), (wr, fr, ar) = left, right
    a = jnp.maximum(al, ar)
    return [(fl[k] + fr[k]) - a * (wr[k] - wl[k]) for k in range(5)]


def cell(prim, d):
    return side(prim, state(prim), sound(prim), d)


def iota(shape, dim):
    return lax.broadcasted_iota(jnp.int32, shape, dim)


def comm_kernel(den, vel, pre, own_hbm, w_out, d_out, r_out, table, U, hs, hr, cm, cr, ms, mr, cs, xs, oh, ps, own, in_sem, hs_sem,
                hr_sem, xs_sem, xr_sem, loc_sem, as_sem, ar_sem, back, last, go):
    me = lax.axis_index("slab")
    sect = lax.axis_index("sect")
    far, row_y, row_z = me // 32, lax.rem(me // 8, 4), lax.rem(me, 8)
    low, second, third = row_z < 4, (row_z >= 4) & (far == 0), (row_z >= 4) & (far == 1)

    owned = pltpu.make_async_copy(own_hbm, own, in_sem.at[3])
    inner = (pl.ds(1, NXL), pl.ds(8, CY))
    copies = [
        pltpu.make_async_copy(den, U.at[(0,) + inner], in_sem.at[0]),
        pltpu.make_async_copy(vel, U.at[(pl.ds(1, 3),) + inner], in_sem.at[1]),
        pltpu.make_async_copy(pre, U.at[(4,) + inner], in_sem.at[2]),
    ]
    for c in copies:
        c.start()
    owned.start()

    def slab_of(step_x, step_y, z):
        return lax.rem(far + step_x, 2) * 32 + lax.rem(row_y + step_y, 4) * 8 + z

    barrier = pltpu.get_barrier_semaphore()
    for i in range(1, NSECT):
        pl.semaphore_signal(barrier, inc=1, device_id={"sect": lax.rem(sect + i, NSECT)}, device_id_type=MESH)

    def tell(sem, q):
        pl.semaphore_signal(sem, inc=1, device_id={"slab": q}, device_id_type=MESH)

    def whole_ring(start, z_from):
        return [start * 32 + lax.rem(row_y + b, 4) * 8 + z for b in (2, 1, 3, 0) for z in range(z_from, z_from + 4)]

    def other_low():
        return [slab_of(a, b, z) for a, b in RINGS for z in range(4)]

    def other_high():
        own = [4 + lax.rem(row_z + i, 4) for i in range(1, 4)]
        return [slab_of(0, b, z) for b in (2, 1, 3) for z in range(4, 8)] + [slab_of(0, 0, z) for z in own]

    @pl.when(low)
    def _():
        for i in range(1, 4):
            tell(barrier, slab_of(0, 0, lax.rem(row_z + i, 4)))
        for q in other_low() + whole_ring(0, 4) + whole_ring(1, 4):
            tell(barrier, q)

    @pl.when(second)
    def _():
        for q in whole_ring(1, 4):
            tell(barrier, q)

    owned.wait()
    row = jnp.concatenate([own[k].astype(F32) for k in range(4)], axis=1)
    across = jnp.broadcast_to(row, (128, 128))
    down = jnp.transpose(across)
    lane, sub = iota((128, 128), 1), iota((128, 128), 0)
    count = lambda i: lax.rem(i, 32) * 4 + i // 32
    earlier = jnp.where((across == down) & (count(sub) < count(lane)), 1.0, 0.0)
    rank = jnp.sum(earlier, axis=0, keepdims=True)
    target = row * MOST + rank
    slots = iota((NSLAB * MOST, 128), 0).astype(F32)
    oh[...] = jnp.where(slots == target, 1.0, 0.0).astype(jnp.bfloat16)

    for c in copies:
        c.wait()

    l8, s8 = iota((8, 128), 1), iota((8, 128), 0)
    pick = lax.rem(l8, 32) == s8 + 8
    for f in range(5):
        for way, y in ((0, 39), (1, 8)):
            edge = U[f, 1:9, y, :]
            hs[way, f] = edge
            turned = pltpu.roll(edge, 8, 1, stride=1, stride_axis=0)
            cm[way, f:f + 1, :] = jnp.sum(jnp.where(pick, turned, 0.0), axis=0, keepdims=True)

    def local_max(x, best):
        for yb in range(4):
            prim = [U[f, x + 1, 8 + 8 * yb:16 + 8 * yb, :] for f in range(5)]
            top = jnp.maximum(jnp.maximum(jnp.abs(prim[1]), jnp.abs(prim[2])), jnp.abs(prim[3])) + sound(prim)
            best = jnp.maximum(best, top)
        return best

    best = lax.fori_loop(0, NXL, local_max, jnp.zeros((8, 128), F32))
    best = jnp.broadcast_to(jnp.max(best, keepdims=True), (8, 128))
    ms[...] = best
    for way in range(2):
        cm[way, 5:8, :] = best[5:8, :]

    pl.semaphore_wait(barrier, 34 + (row_z // 4) * (1 + 16 * far))

    def remote(src, dst, ssem, rsem, where):
        return pltpu.make_async_remote_copy(src_ref=src, dst_ref=dst, send_sem=ssem, recv_sem=rsem, device_id=where,
                                            device_id_type=MESH)

    above_me, below_me = {"sect": lax.rem(sect + 1, NSECT)}, {"sect": lax.rem(sect + NSECT - 1, NSECT)}
    near = [
        remote(cm.at[0], cr.at[0], hs_sem.at[0], hr_sem.at[0], above_me),
        remote(cm.at[1], cr.at[1], hs_sem.at[1], hr_sem.at[1], below_me),
        remote(ms, mr, hs_sem.at[2], hr_sem.at[2], {"sect": lax.rem(sect + 2, NSECT)}),
    ]
    sides = [
        remote(hs.at[0], hr.at[0], hs_sem.at[3], hr_sem.at[3], above_me),
        remote(hs.at[1], hr.at[1], hs_sem.at[4], hr_sem.at[4], below_me),
    ]
    after, before = lax.rem(me + 1, NSLAB), lax.rem(me + NSLAB - 1, NSLAB)
    ends = [
        remote(U.at[:, 8, pl.ds(8, CY)], U.at[:, 0, pl.ds(8, CY)], xs_sem.at[0], xr_sem.at[0], {"slab": after}),
        remote(U.at[:, 1, pl.ds(8, CY)], U.at[:, 9, pl.ds(8, CY)], xs_sem.at[1], xr_sem.at[1], {"slab": before}),
    ]
    for c in near + sides:
        c.start()

    @pl.when(second)
    def _():
        for q in whole_ring(0, 0) + whole_ring(1, 0):
            tell(back, q)

    @pl.when(third)
    def _():
        for q in whole_ring(0, 0) + whole_ring(1, 0) + whole_ring(0, 4):
            tell(last, q)

    @pl.when((row_z < 3) | (row_z == 7))
    def _():
        ends[0].start()

    @pl.when((row_z > 0) & (row_z < 4))
    def _():
        ends[1].start()

    wide = iota((CY, 128), 1)
    wide32 = lax.rem(wide, 32)
    for f in range(5):
        packed = jnp.ones((CY, 128), F32)
        for x in range(NXL):
            tile = U[f, x + 1, 8:40, :]
            for step in (-1, 0, 1):
                n = x + 8 * (step + 1)
                shift = (n - step) % 128
                packed = jnp.where(wide32 == n, pltpu.roll(tile, shift, 1) if shift else tile, packed)
        cs[f, 8:40, :] = packed

    for c in near:
        c.wait_recv()
    best = jnp.maximum(jnp.maximum(best[5:6, :], cr[0, 5:6, :]), jnp.maximum(cr[1, 5:6, :], mr[5:6, :]))
    for f in range(5):
        cs[f, 7:8, :] = cr[0, f:f + 1, :]
        cs[f, 40:41, :] = cr[1, f:f + 1, :]

    l8_32 = lax.rem(l8, 32)
    middle = (l8_32 >= 8) & (l8_32 < 16)
    for yb in range(4):
        here = [cs[f, 8 + 8 * yb:16 + 8 * yb, :] for f in range(5)]
        above = [cs[f, 9 + 8 * yb:17 + 8 * yb, :] for f in range(5)]
        below = [cs[f, 7 + 8 * yb:15 + 8 * yb, :] for f in range(5)]
        w, c = state(here), sound(here)
        nextz = [pltpu.roll(a, 120, 1) for a in here]
        fz = face(side(here, w, c, 2), cell(nextz, 2))
        mid = side(here, w, c, 1)
        fu, fd = face(mid, cell(above, 1)), face(cell(below, 1), mid)
        moved = [(fu[k] - fd[k]) + (fz[k] - pltpu.roll(fz[k], 8, 1)) for k in range(5)]
        items = [jnp.where(middle, a, 0.0) for a in list(here) + moved]
        groups = []
        for g in range(3):
            total = None
            for j, item in enumerate(items[4 * g:4 * g + 4]):
                shift = (8 * j - 8) % 128
                part = pltpu.roll(item, shift, 1) if shift else item
                total = part if total is None else total + part
            groups.append(total)
        for k in range(4):
            block = jnp.zeros((8, 128), F32)
            for g in range(3):
                shift = (32 * g - 32 * k) % 128
                part = pltpu.roll(groups[g], shift, 1) if shift else groups[g]
                block = jnp.where(l8 // 32 == g, part, block)
            xs[32 * k + 8 * yb:32 * k + 8 * yb + 8, :] = block

    lines = xs[...]
    hi = lines.astype(jnp.bfloat16)
    rest = lines - hi.astype(F32)
    mid = rest.astype(jnp.bfloat16)
    lo = (rest - mid.astype(F32)).astype(jnp.bfloat16)
    chosen = oh[...]
    dot = functools.partial(jnp.dot, preferred_element_type=F32)
    sent = dot(chosen, hi) + (dot(chosen, mid) + dot(chosen, lo))
    sent = jnp.where(iota((NSLAB * MOST, 128), 1) >= 80, jnp.broadcast_to(best, (NSLAB * MOST, 128)), sent)
    ps[...] = sent.reshape(NSLAB, MOST, 128)

    def deliver(q):
        remote(ps.at[q], r_out.at[me], as_sem, ar_sem, {"slab": q}).start()

    @pl.when(low)
    def _():
        for q in other_low() + [slab_of(0, 0, lax.rem(row_z + i, 4)) for i in range(1, 4)]:
            deliver(q)
        pl.semaphore_wait(back, NSLAB // 4)

        @pl.when((far == 0) & (row_z == 3))
        def _():
            tell(go, slab_of(0, 0, 4))
            tell(go, slab_of(0, 0, 5))

        @pl.when((far == 0) & (row_z == 0))
        def _():
            tell(go, slab_of(0, 0, 6))
            tell(go, slab_of(0, 0, 7))

        for q in whole_ring(0, 4):
            deliver(q)
        pl.semaphore_wait(last, NSLAB // 4)

        @pl.when(row_z == 3)
        def _():
            ends[0].start()

        @pl.when(row_z == 0)
        def _():
            ends[1].start()

        for q in whole_ring(1, 4):
            deliver(q)

    def to_low():
        for q in [slab_of(a, b, z) for a, b in RINGS + ((0, 0),) for z in range(4)]:
            deliver(q)

        @pl.when(row_z == 4)
        def _():
            ends[1].start()

    def to_own():
        @pl.when(row_z < 7)
        def _():
            ends[0].start()

        @pl.when(row_z > 4)
        def _():
            ends[1].start()

        for q in other_high():
            deliver(q)

    @pl.when(second)
    def _():
        to_low()
        pl.semaphore_wait(go, 1)
        to_own()
        pl.semaphore_wait(last, NSLAB // 4)
        tell(go, me + 32)
        for q in whole_ring(1, 4):
            deliver(q)

    @pl.when(third)
    def _():
        to_low()
        for q in whole_ring(0, 4):
            deliver(q)
        pl.semaphore_wait(go, 1)
        to_own()

    mine = pltpu.make_async_copy(ps.at[me], r_out.at[me], loc_sem)
    mine.start()

    for u in range(65):
        o = s8 + (8 * u - 8) - 8 * (l8 // 4)
        o = jnp.where(o >= NX // 2, o - NX, o)
        table[8 * u:8 * u + 8, :] = o.astype(F32)

    for c in sides:
        c.wait_recv()
    for f in range(5):
        U[f, 1:9, 7, :] = hr[0, f]
        U[f, 1:9, 40, :] = hr[1, f]

    def dense(x, carry):
        for yb in range(4):
            lo, hi = 8 + 8 * yb, 16 + 8 * yb
            here = [U[f, x + 1, lo:hi, :] for f in range(5)]
            w, c = state(here), sound(here)
            fz = face(side(here, w, c, 2), cell([pltpu.roll(a, 127, 1) for a in here], 2))
            moved = [fz[k] - pltpu.roll(fz[k], 1, 1) for k in range(5)]
            for d, pair in ((1, ((1, 1), (1, -1))), (0, ((2, 0), (0, 0)))):
                (xu, yu), (xd, yd) = pair
                mid = side(here, w, c, d)
                fu = face(mid, cell([U[f, x + xu, lo + yu:hi + yu, :] for f in range(5)], d))
                fd = face(cell([U[f, x + xd, lo + yd:hi + yd, :] for f in range(5)], d), mid)
                moved = [moved[k] + (fu[k] - fd[k]) for k in range(5)]
            for k in range(5):
                w_out[k, x, lo - 8:hi - 8, :] = w[k]
                d_out[k, x, lo - 8:hi - 8, :] = moved[k]
        return carry

    lax.fori_loop(1, NXL - 1, dense, 0)
    for c in ends:
        c.wait_recv()
    lax.fori_loop(0, 2, lambda i, carry: dense((NXL - 1) * i, carry), 0)

    mine.wait()
    for c in near + sides + ends:
        c.wait_send()
    most = pl.ds(0, NSLAB - 1)
    pltpu.make_async_copy(ps.at[most], ps.at[most], as_sem).wait()
    pltpu.make_async_copy(r_out.at[most], r_out.at[most], ar_sem).wait()


def final_kernel(w_ref, d_ref, r_ref, table, own_hbm, new_hbm, od, nb, pb, acc, own, sem, own_sem):
    me = lax.axis_index("slab").astype(F32)
    owned = pltpu.make_async_copy(own_hbm, own, own_sem)
    owned.start()
    arrived = r_ref[...]
    fastest = jnp.max(jnp.max(arrived, axis=0), axis=0, keepdims=True)[:, 96:97]
    half_dt = (0.5 * COURANT) / fastest
    hdt = jnp.broadcast_to(half_dt, (8, 128))

    outs = []
    for k in range(5):
        for x in range(NXL):
            for yb in range(4):
                at = (k, x, slice(8 * yb, 8 * yb + 8))
                nb[at] = w_ref[at] - hdt * d_ref[at]
        outs.append(pltpu.make_async_copy(nb.at[k], new_hbm.at[k], sem.at[k]))
        outs[-1].start()

    turned = jnp.transpose(arrived.reshape(NSLAB * MOST, 128))
    fields = [turned[8 * f:8 * f + 8, :] for f in range(10)]
    here, moved = fields[:5], fields[5:]
    s2 = iota((8, NSLAB * MOST), 0)

    def after(a):
        a = pltpu.roll(a, 7, 0)
        return jnp.where(s2 < 7, a, pltpu.roll(a, NSLAB * MOST - 4, 1))

    def before(a):
        a = pltpu.roll(a, 1, 0)
        return jnp.where(s2 > 0, a, pltpu.roll(a, 4, 1))

    w = state(here)
    fx = face(side(here, w, sound(here), 0), cell([after(a) for a in here], 0))
    hdt2 = jnp.broadcast_to(half_dt, (8, NSLAB * MOST))
    new = [w[k] - hdt2 * (moved[k] + (fx[k] - before(fx[k]))) for k in range(5)]
    r = new[0]
    v = [new[1 + k] / r for k in range(3)]
    p = (GAMMA - 1.0) * (new[4] - 0.5 * (new[1] * v[0] + new[2] * v[1] + new[3] * v[2]))
    broad = TURBULENT + p / r
    inverse = math.sqrt(LOG2E) / (8.0 * jnp.sqrt(broad))
    moved_by = (64.0 * v[0]) * inverse
    level = jnp.log2((NORMALISE / 8.0) * (r * r)) - 1.2 * jnp.log2(broad)
    for n, param in enumerate((inverse, moved_by, level)):
        for h in range(2):
            for x in range(8):
                pb[n, 8 * h + x] = jnp.broadcast_to(param[x:x + 1, 128 * h:128 * h + 128], (8, 128))

    def pixels(block, carry):
        first = pl.multiple_of(64 * block, 64)
        starts = (first, pl.multiple_of(lax.rem(first + NX // 2, NX), 64))
        sums = [None] * 8
        for h in range(2):
            for x in range(8):
                inv, mov, lev = (pb[n, 8 * h + x] for n in range(3))
                for j in range(8):
                    o = table[pl.ds(starts[h] + (8 * j + 8 - x), 8), :]
                    z = o * inv - mov
                    part = jnp.exp2(lev - z * z)
                    sums[j] = part if sums[j] is None else sums[j] + part
        for j in range(8):
            acc[pl.ds(first + 8 * j, 8), :] = sums[j]
        return carry

    lax.fori_loop(0, 8, pixels, 0)
    depth = jnp.transpose(acc[...])
    both = depth[0:8, :]
    for n in range(1, 16):
        both = both + depth[8 * n:8 * n + 8, :]
    owned.wait()
    row = jnp.concatenate([own[k].astype(F32) for k in range(4)], axis=1)
    held = jnp.sum(jnp.where(row == me, 1.0, 0.0), axis=1, keepdims=True)
    valid = iota((4, NX), 0).astype(F32) < held
    od[0, 0] = jnp.where(valid, both[0:4, :] + both[4:8, :], 0.0)
    for out in outs:
        out.wait()


def body(density, velocity, pressure, owners):
    own = jnp.transpose(owners, (1, 2, 0))
    density, velocity, pressure, own = (pltpu.with_memory_space_constraint(a, pltpu.HBM) for a in (density, velocity, pressure, own))
    vmem = pl.BlockSpec(memory_space=pltpu.VMEM)
    hbm = pl.BlockSpec(memory_space=pltpu.HBM)
    dense = jax.ShapeDtypeStruct((5, NXL, CY, NZ), F32)
    arrived = jax.ShapeDtypeStruct((NSLAB, MOST, 128), F32)
    offsets = jax.ShapeDtypeStruct((NX + 8, 128), F32)
    dma, regular = pltpu.SemaphoreType.DMA, pltpu.SemaphoreType.REGULAR
    w, d, r, table = pl.pallas_call(
        comm_kernel,
        out_shape=(dense, dense, arrived, offsets),
        in_specs=[hbm, hbm, hbm, hbm],
        out_specs=(vmem, vmem, vmem, vmem),
        scratch_shapes=[
            pltpu.VMEM((5, NXL + 2, CY + 16, NZ), F32),
            pltpu.VMEM((2, 5, 8, 128), F32),
            pltpu.VMEM((2, 5, 8, 128), F32),
            pltpu.VMEM((2, 8, 128), F32),
            pltpu.VMEM((2, 8, 128), F32),
            pltpu.VMEM((8, 128), F32),
            pltpu.VMEM((8, 128), F32),
            pltpu.VMEM((5, CY + 16, 128), F32),
            pltpu.VMEM((128, 128), F32),
            pltpu.VMEM((NSLAB * MOST, 128), jnp.bfloat16),
            pltpu.VMEM((NSLAB, MOST, 128), F32),
            pltpu.VMEM((4, 1, CY), jnp.int32),
            dma((4,)), dma((5,)), dma((5,)), dma((2,)), dma((2,)), dma, dma, dma, regular, regular, regular,
        ],
        compiler_params=pltpu.CompilerParams(collective_id=0, has_side_effects=True, vmem_limit_bytes=24 << 20),
        name="exchange",
    )(density, velocity, pressure, own)
    return tuple(pl.pallas_call(
        final_kernel,
        out_shape=(dense, jax.ShapeDtypeStruct((1, 1, MOST, NX), F32)),
        in_specs=[vmem, vmem, vmem, vmem, hbm],
        out_specs=(hbm, vmem),
        scratch_shapes=[
            pltpu.VMEM((5, NXL, CY, NZ), F32),
            pltpu.VMEM((3, 16, 8, 128), F32),
            pltpu.VMEM((NX, 128), F32),
            pltpu.VMEM((4, 1, CY), jnp.int32),
            dma((5,)), dma,
        ],
        compiler_params=pltpu.CompilerParams(vmem_limit_bytes=24 << 20),
        name="finish",
    )(w, d, r, table, own))


def solution(mesh):
    placed = (P("slab", "sect", None), P(None, "slab", "sect", None), P("slab", "sect", None), P("sect", None, None))
    return jax.shard_map(body, mesh=mesh, in_specs=placed, out_specs=(P(None, "slab", "sect", None), P("sect", "slab", None, None)),
                         check_vma=False)
```

```python
import functools
import math

import jax
import jax.numpy as jnp
from jax import lax
from jax.experimental import pallas as pl
from jax.experimental.pallas import tpu as pltpu
from jax.sharding import PartitionSpec as P

MESH = pl.DeviceIdType.MESH
GAMMA = 5.0 / 3.0
COURANT = 0.15
TURBULENT = 0.25
NORMALISE = 0.5641895835477563
NSLAB = 64
NSECT = 4
NXL = 8
CY = 32
NZ = 128
MOST = 4
NX = 512
F32 = jnp.float32
LOG2E = math.log2(math.e)
HOPS = lambda a, b, c: 2 * a + min(b, 4 - b) + min(c, 8 - c)
PARTNERS = sorted(((a, b, c) for a in range(2) for b in range(4) for c in range(8) if a + b + c), key=lambda o: -HOPS(*o))
HUB = 53
FROM_HUB = sorted((q for q in range(NSLAB) if q != HUB),
                  key=lambda q: HOPS((q // 32 - 1) % 2, (q // 8 % 4 - 2) % 4, (q % 8 - 5) % 8))


def state(prim):
    r, v0, v1, v2, p = prim
    m0, m1, m2 = r * v0, r * v1, r * v2
    energy = 1.5 * p + 0.5 * (m0 * v0 + m1 * v1 + m2 * v2)
    return (r, m0, m1, m2, energy)


def sound(prim):
    return jnp.sqrt(GAMMA * (prim[4] / prim[0]))


def side(prim, w, c, d):
    moving, p = prim[1 + d], prim[4]
    flux = [w[1 + d], w[1] * moving, w[2] * moving, w[3] * moving, (w[4] + p) * moving]
    flux[1 + d] = flux[1 + d] + p
    return w, flux, jnp.abs(moving) + c


def face(left, right):
    (wl, fl, al), (wr, fr, ar) = left, right
    a = jnp.maximum(al, ar)
    return [(fl[k] + fr[k]) - a * (wr[k] - wl[k]) for k in range(5)]


def cell(prim, d):
    return side(prim, state(prim), sound(prim), d)


def iota(shape, dim):
    return lax.broadcasted_iota(jnp.int32, shape, dim)


def comm_kernel(den, vel, pre, own_hbm, w_out, d_out, r_out, table, U, hs, hr, cm, cr, ms, mr, cs, xs, oh, ohc, base, ps, own, in_sem, hs_sem,
                hr_sem, xs_sem, xr_sem, loc_sem, as_sem, ar_sem, go):
    me = lax.axis_index("slab")
    sect = lax.axis_index("sect")
    far, row_y, row_z = me // 32, lax.rem(me // 8, 4), lax.rem(me, 8)
    owned = pltpu.make_async_copy(own_hbm, own, in_sem.at[6])
    copies = []
    for half in range(2):
        some, to = pl.ds(4 * half, 4), (pl.ds(1 + 4 * half, 4), pl.ds(8, CY))
        copies += [
            pltpu.make_async_copy(den.at[some], U.at[(0,) + to], in_sem.at[3 * half]),
            pltpu.make_async_copy(vel.at[:, some], U.at[(pl.ds(1, 3),) + to], in_sem.at[3 * half + 1]),
            pltpu.make_async_copy(pre.at[some], U.at[(4,) + to], in_sem.at[3 * half + 2]),
        ]
    for c in copies:
        c.start()
    owned.start()

    def slab_of(step_x, step_y, z):
        return lax.rem(far + step_x, 2) * 32 + lax.rem(row_y + step_y, 4) * 8 + z

    barrier = pltpu.get_barrier_semaphore()
    for i in range(1, NSECT):
        pl.semaphore_signal(barrier, inc=1, device_id={"sect": lax.rem(sect + i, NSECT)}, device_id_type=MESH)

    def tell(sem, q):
        pl.semaphore_signal(sem, inc=1, device_id={"slab": q}, device_id_type=MESH)

    after, before = lax.rem(me + 1, NSLAB), lax.rem(me + NSLAB - 1, NSLAB)

    @pl.when(me != HUB)
    def _():
        tell(barrier, HUB)

    @pl.when(after != HUB)
    def _():
        tell(barrier, after)

    @pl.when(before != HUB)
    def _():
        tell(barrier, before)

    @pl.when(me == HUB)
    def _():
        pl.semaphore_wait(barrier, NSLAB - 1 + NSECT - 1)
        for q in FROM_HUB:
            tell(go, q)

    best = jnp.zeros((8, 128), F32)
    for half in range(2):
        for c in copies[3 * half:3 * half + 3]:
            c.wait()
        for x in range(4 * half, 4 * half + 4):
            for yb in range(4):
                prim = [U[f, x + 1, 8 + 8 * yb:16 + 8 * yb, :] for f in range(5)]
                top = jnp.maximum(jnp.maximum(jnp.abs(prim[1]), jnp.abs(prim[2])), jnp.abs(prim[3])) + sound(prim)
                best = jnp.maximum(best, top)
    best = jnp.broadcast_to(jnp.max(best, keepdims=True), (8, 128))
    l8, s8 = iota((8, 128), 1), iota((8, 128), 0)
    pick = lax.rem(l8, 32) == s8 + 8
    for f in range(5):
        for way, y in ((0, 39), (1, 8)):
            edge = U[f, 1:9, y, :]
            hs[way, f] = edge
            turned = pltpu.roll(edge, 8, 1, stride=1, stride_axis=0)
            cm[way, f:f + 1, :] = jnp.sum(jnp.where(pick, turned, 0.0), axis=0, keepdims=True)
    for way in range(2):
        cm[way, 5:8, :] = best[5:8, :]
    ms[...] = best

    @pl.when(me != HUB)
    def _():
        pl.semaphore_wait(barrier, NSECT + 1)

    def remote(src, dst, ssem, rsem, where):
        return pltpu.make_async_remote_copy(src_ref=src, dst_ref=dst, send_sem=ssem, recv_sem=rsem, device_id=where,
                                            device_id_type=MESH)

    sects = [{"sect": lax.rem(sect + i, NSECT)} for i in range(NSECT)]
    near = [
        remote(cm.at[0], cr.at[0], hs_sem.at[0], hr_sem.at[0], sects[1]),
        remote(cm.at[1], cr.at[1], hs_sem.at[1], hr_sem.at[1], sects[3]),
        remote(ms, mr, hs_sem.at[2], hr_sem.at[2], sects[2]),
    ]
    sides = [
        remote(hs.at[0], hr.at[0], hs_sem.at[3], hr_sem.at[3], sects[1]),
        remote(hs.at[1], hr.at[1], hs_sem.at[4], hr_sem.at[4], sects[3]),
    ]
    ends = [
        remote(U.at[:, 8, pl.ds(8, CY)], U.at[:, 0, pl.ds(8, CY)], xs_sem.at[0], xr_sem.at[0], {"slab": after}),
        remote(U.at[:, 1, pl.ds(8, CY)], U.at[:, 9, pl.ds(8, CY)], xs_sem.at[1], xr_sem.at[1], {"slab": before}),
    ]
    for c in near + sides + ends:
        c.start()

    owned.wait()
    row = jnp.concatenate([own[k].astype(F32) for k in range(4)], axis=1)
    across = jnp.broadcast_to(row, (128, 128))
    down = jnp.transpose(across)
    lane, sub = iota((128, 128), 1), iota((128, 128), 0)
    count = lambda i: lax.rem(i, 32) * 4 + i // 32
    earlier = jnp.where((across == down) & (count(sub) < count(lane)), 1.0, 0.0)
    rank = jnp.sum(earlier, axis=0, keepdims=True)
    target = row * MOST + rank
    slots = iota((NSLAB * MOST, 128), 0).astype(F32)
    oh[...] = jnp.where(slots == target, 1.0, 0.0).astype(jnp.bfloat16)
    target8, edges = jnp.broadcast_to(target, (8, 128)), jnp.full((8, 128), -1.0, F32)
    for part in range(3):
        for k in range(4):
            for e in range(2):
                to, source = 32 * part + 8 * k + e, 32 * k + 31 * e
                shift = (to - source) % 128
                edges = jnp.where(l8 == to, pltpu.roll(target8, shift, 1) if shift else target8, edges)
    ohc[...] = jnp.where(slots == edges[0:1, :], 1.0, 0.0).astype(jnp.bfloat16)

    wide = iota((CY, 128), 1)
    wide32 = lax.rem(wide, 32)
    for f in range(5):
        packed = jnp.ones((CY, 128), F32)
        for x in range(NXL):
            tile = U[f, x + 1, 8:40, :]
            for step in (-1, 0, 1):
                n = x + 8 * (step + 1)
                shift = (n - step) % 128
                packed = jnp.where(wide32 == n, pltpu.roll(tile, shift, 1) if shift else tile, packed)
        cs[f, 8:40, :] = packed
        cs[f, 7:8, :] = jnp.ones((1, 128), F32)
        cs[f, 40:41, :] = jnp.ones((1, 128), F32)

    middle = (lax.rem(l8, 32) >= 8) & (lax.rem(l8, 32) < 16)

    def gather_fields(items):
        total = None
        for j, item in items:
            shift = (8 * j - 8) % 128
            item = jnp.where(middle, item, 0.0)
            part = pltpu.roll(item, shift, 1) if shift else item
            total = part if total is None else total + part
        return total

    def of_line(groups, k):
        block = jnp.zeros((8, 128), F32)
        for g, group in groups.items():
            shift = (32 * g - 32 * k) % 128
            block = jnp.where(l8 // 32 == g, pltpu.roll(group, shift, 1) if shift else group, block)
        return block

    for yb in range(4):
        here = [cs[f, 8 + 8 * yb:16 + 8 * yb, :] for f in range(5)]
        above = [cs[f, 9 + 8 * yb:17 + 8 * yb, :] for f in range(5)]
        below = [cs[f, 7 + 8 * yb:15 + 8 * yb, :] for f in range(5)]
        w, c = state(here), sound(here)
        fz = face(side(here, w, c, 2), cell([pltpu.roll(a, 120, 1) for a in here], 2))
        centre = side(here, w, c, 1)
        fu, fd = face(centre, cell(above, 1)), face(cell(below, 1), centre)
        if yb == 0:
            fd = [jnp.where(s8 == 0, 0.0, a) for a in fd]
        if yb == 3:
            fu = [jnp.where(s8 == 7, 0.0, a) for a in fu]
        moved = [(fu[k] - fd[k]) + (fz[k] - pltpu.roll(fz[k], 8, 1)) for k in range(5)]
        items = list(here) + moved
        groups = {g: gather_fields(list(enumerate(items[4 * g:4 * g + 4]))) for g in range(3)}
        for k in range(4):
            xs[32 * k + 8 * yb:32 * k + 8 * yb + 8, :] = of_line(groups, k)

    def parts(a):
        hi = a.astype(jnp.bfloat16)
        rest = a - hi.astype(F32)
        mid = rest.astype(jnp.bfloat16)
        return hi, mid, (rest - mid.astype(F32)).astype(jnp.bfloat16)

    dot = functools.partial(jnp.dot, preferred_element_type=F32)
    hi, mid, lo = parts(xs[...])
    chosen = oh[...]
    base[...] = dot(chosen, hi) + (dot(chosen, mid) + dot(chosen, lo))

    for u in range(65):
        o = s8 + (8 * u - 8) - 8 * (l8 // 4)
        o = jnp.where(o >= NX // 2, o - NX, o)
        table[8 * u:8 * u + 8, :] = o.astype(F32)

    for c in near:
        c.wait_recv()
    first = s8 == 0
    left, right = [], []
    for f in range(5):
        wide8 = lambda a: jnp.broadcast_to(a, (8, 128))
        left.append(jnp.where(first, wide8(cr[0, f:f + 1, :]), wide8(cs[f, 39:40, :])))
        right.append(jnp.where(first, wide8(cs[f, 8:9, :]), wide8(cr[1, f:f + 1, :])))
    fe = [jnp.where(first, -a, a) for a in face(cell(left, 1), cell(right, 1))]
    groups = {1: gather_fields(list(enumerate(fe[:3], 1))), 2: gather_fields(list(enumerate(fe[3:])))}
    extra = parts(jnp.concatenate([of_line(groups, k) for k in range(4)], axis=0))
    blank = jnp.zeros((32, 128), jnp.bfloat16)
    added = dot(ohc[...], jnp.concatenate(list(extra) + [blank], axis=0))
    best = jnp.maximum(jnp.maximum(best, mr[...])[5:6, :], jnp.maximum(cr[0, 5:6, :], cr[1, 5:6, :]))
    sent = jnp.where(iota((NSLAB * MOST, 128), 1) >= 80, jnp.broadcast_to(best, (NSLAB * MOST, 128)), base[...] + added)
    ps[...] = sent.reshape(NSLAB, MOST, 128)

    def deliver(q):
        remote(ps.at[q], r_out.at[me], as_sem, ar_sem, {"slab": q}).start()

    @pl.when(me != HUB)
    def _():
        pl.semaphore_wait(go, 1)

    for a, b, c in PARTNERS:
        deliver(slab_of(a, b, lax.rem(row_z + c, 8)))
    mine = pltpu.make_async_copy(ps.at[me], r_out.at[me], loc_sem)
    mine.start()

    for c in sides:
        c.wait_recv()
    for f in range(5):
        U[f, 1:9, 7, :] = hr[0, f]
        U[f, 1:9, 40, :] = hr[1, f]

    def dense(x, carry):
        for yb in range(4):
            lo, hi = 8 + 8 * yb, 16 + 8 * yb
            here = [U[f, x + 1, lo:hi, :] for f in range(5)]
            w, c = state(here), sound(here)
            fz = face(side(here, w, c, 2), cell([pltpu.roll(a, 127, 1) for a in here], 2))
            moved = [fz[k] - pltpu.roll(fz[k], 1, 1) for k in range(5)]
            for d, pair in ((1, ((1, 1), (1, -1))), (0, ((2, 0), (0, 0)))):
                (xu, yu), (xd, yd) = pair
                mid = side(here, w, c, d)
                fu = face(mid, cell([U[f, x + xu, lo + yu:hi + yu, :] for f in range(5)], d))
                fd = face(cell([U[f, x + xd, lo + yd:hi + yd, :] for f in range(5)], d), mid)
                moved = [moved[k] + (fu[k] - fd[k]) for k in range(5)]
            for k in range(5):
                w_out[k, x, lo - 8:hi - 8, :] = w[k]
                d_out[k, x, lo - 8:hi - 8, :] = moved[k]
        return carry

    lax.fori_loop(1, NXL - 1, dense, 0)
    for c in ends:
        c.wait_recv()
    lax.fori_loop(0, 2, lambda i, carry: dense((NXL - 1) * i, carry), 0)

    mine.wait()
    for c in near + sides + ends:
        c.wait_send()
    most = pl.ds(0, NSLAB - 1)
    pltpu.make_async_copy(ps.at[most], ps.at[most], as_sem).wait()
    pltpu.make_async_copy(r_out.at[most], r_out.at[most], ar_sem).wait()


def final_kernel(w_ref, d_ref, r_ref, table, own_hbm, new_hbm, od, nb, pb, acc, own, sem, own_sem):
    me = lax.axis_index("slab").astype(F32)
    owned = pltpu.make_async_copy(own_hbm, own, own_sem)
    owned.start()
    arrived = r_ref[...]
    fastest = jnp.max(jnp.max(arrived, axis=0), axis=0, keepdims=True)[:, 96:97]
    half_dt = (0.5 * COURANT) / fastest
    hdt = jnp.broadcast_to(half_dt, (8, 128))

    outs = []
    for k in range(5):
        for x in range(NXL):
            for yb in range(4):
                at = (k, x, slice(8 * yb, 8 * yb + 8))
                nb[at] = w_ref[at] - hdt * d_ref[at]
        outs.append(pltpu.make_async_copy(nb.at[k], new_hbm.at[k], sem.at[k]))
        outs[-1].start()

    turned = jnp.transpose(arrived.reshape(NSLAB * MOST, 128))
    fields = [turned[8 * f:8 * f + 8, :] for f in range(10)]
    here, moved = fields[:5], fields[5:]
    s2 = iota((8, NSLAB * MOST), 0)

    def after(a):
        a = pltpu.roll(a, 7, 0)
        return jnp.where(s2 < 7, a, pltpu.roll(a, NSLAB * MOST - 4, 1))

    def before(a):
        a = pltpu.roll(a, 1, 0)
        return jnp.where(s2 > 0, a, pltpu.roll(a, 4, 1))

    w = state(here)
    fx = face(side(here, w, sound(here), 0), cell([after(a) for a in here], 0))
    hdt2 = jnp.broadcast_to(half_dt, (8, NSLAB * MOST))
    new = [w[k] - hdt2 * (moved[k] + (fx[k] - before(fx[k]))) for k in range(5)]
    r = new[0]
    v = [new[1 + k] / r for k in range(3)]
    p = (GAMMA - 1.0) * (new[4] - 0.5 * (new[1] * v[0] + new[2] * v[1] + new[3] * v[2]))
    broad = TURBULENT + p / r
    inverse = math.sqrt(LOG2E) / (8.0 * jnp.sqrt(broad))
    moved_by = (64.0 * v[0]) * inverse
    level = jnp.log2((NORMALISE / 8.0) * (r * r)) - 1.2 * jnp.log2(broad)
    for n, param in enumerate((inverse, moved_by, level)):
        for h in range(2):
            for x in range(8):
                pb[n, 8 * h + x] = jnp.broadcast_to(param[x:x + 1, 128 * h:128 * h + 128], (8, 128))

    def pixels(block, carry):
        first = pl.multiple_of(128 * block, 128)
        starts = (first, pl.multiple_of(lax.rem(first + NX // 2, NX), 128))
        sums = [None] * 16
        for h in range(2):
            for x in range(8):
                inv, mov, lev = (pb[n, 8 * h + x] for n in range(3))
                for j in range(16):
                    o = table[pl.ds(starts[h] + (8 * j + 8 - x), 8), :]
                    z = o * inv - mov
                    part = jnp.exp2(lev - z * z)
                    sums[j] = part if sums[j] is None else sums[j] + part
        for j in range(16):
            acc[pl.ds(first + 8 * j, 8), :] = sums[j]
        return carry

    lax.fori_loop(0, 4, pixels, 0)
    depth = jnp.transpose(acc[...])
    both = depth[0:8, :]
    for n in range(1, 16):
        both = both + depth[8 * n:8 * n + 8, :]
    owned.wait()
    row = jnp.concatenate([own[k].astype(F32) for k in range(4)], axis=1)
    held = jnp.sum(jnp.where(row == me, 1.0, 0.0), axis=1, keepdims=True)
    valid = iota((4, NX), 0).astype(F32) < held
    od[0, 0] = jnp.where(valid, both[0:4, :] + both[4:8, :], 0.0)
    for out in outs:
        out.wait()


def body(density, velocity, pressure, owners):
    own = jnp.transpose(owners, (1, 2, 0))
    density, velocity, pressure, own = (pltpu.with_memory_space_constraint(a, pltpu.HBM) for a in (density, velocity, pressure, own))
    vmem = pl.BlockSpec(memory_space=pltpu.VMEM)
    hbm = pl.BlockSpec(memory_space=pltpu.HBM)
    dense = jax.ShapeDtypeStruct((5, NXL, CY, NZ), F32)
    arrived = jax.ShapeDtypeStruct((NSLAB, MOST, 128), F32)
    offsets = jax.ShapeDtypeStruct((NX + 8, 128), F32)
    dma, regular = pltpu.SemaphoreType.DMA, pltpu.SemaphoreType.REGULAR
    w, d, r, table = pl.pallas_call(
        comm_kernel,
        out_shape=(dense, dense, arrived, offsets),
        in_specs=[hbm, hbm, hbm, hbm],
        out_specs=(vmem, vmem, vmem, vmem),
        scratch_shapes=[
            pltpu.VMEM((5, NXL + 2, CY + 16, NZ), F32),
            pltpu.VMEM((2, 5, 8, 128), F32),
            pltpu.VMEM((2, 5, 8, 128), F32),
            pltpu.VMEM((2, 8, 128), F32),
            pltpu.VMEM((2, 8, 128), F32),
            pltpu.VMEM((8, 128), F32),
            pltpu.VMEM((8, 128), F32),
            pltpu.VMEM((5, CY + 16, 128), F32),
            pltpu.VMEM((128, 128), F32),
            pltpu.VMEM((NSLAB * MOST, 128), jnp.bfloat16),
            pltpu.VMEM((NSLAB * MOST, 128), jnp.bfloat16),
            pltpu.VMEM((NSLAB * MOST, 128), F32),
            pltpu.VMEM((NSLAB, MOST, 128), F32),
            pltpu.VMEM((4, 1, CY), jnp.int32),
            dma((7,)), dma((5,)), dma((5,)), dma((2,)), dma((2,)), dma, dma, dma, regular,
        ],
        compiler_params=pltpu.CompilerParams(collective_id=0, has_side_effects=True, vmem_limit_bytes=24 << 20),
        name="exchange",
    )(density, velocity, pressure, own)
    return tuple(pl.pallas_call(
        final_kernel,
        out_shape=(dense, jax.ShapeDtypeStruct((1, 1, MOST, NX), F32)),
        in_specs=[vmem, vmem, vmem, vmem, hbm],
        out_specs=(hbm, vmem),
        scratch_shapes=[
            pltpu.VMEM((5, NXL, CY, NZ), F32),
            pltpu.VMEM((3, 16, 8, 128), F32),
            pltpu.VMEM((NX, 128), F32),
            pltpu.VMEM((4, 1, CY), jnp.int32),
            dma((5,)), dma,
        ],
        compiler_params=pltpu.CompilerParams(vmem_limit_bytes=24 << 20),
        name="finish",
    )(w, d, r, table, own))


def solution(mesh):
    placed = (P("slab", "sect", None), P(None, "slab", "sect", None), P("slab", "sect", None), P("sect", None, None))
    return jax.shard_map(body, mesh=mesh, in_specs=placed, out_specs=(P(None, "slab", "sect", None), P("sect", "slab", None, None)),
                         check_vma=False)
```

```python
import functools
import math

import jax
import jax.numpy as jnp
from jax import lax
from jax.experimental import pallas as pl
from jax.experimental.pallas import tpu as pltpu
from jax.sharding import PartitionSpec as P

MESH = pl.DeviceIdType.MESH
GAMMA = 5.0 / 3.0
COURANT = 0.15
TURBULENT = 0.25
NORMALISE = 0.5641895835477563
NSLAB = 64
NSECT = 4
NXL = 8
CY = 32
NZ = 128
MOST = 4
NX = 512
F32 = jnp.float32
LOG2E = math.log2(math.e)
HOPS = lambda a, b, c: 2 * a + min(b, 4 - b) + min(c, 8 - c)
PARTNERS = sorted(((a, b, c) for a in range(2) for b in range(4) for c in range(8) if a + b + c), key=lambda o: -HOPS(*o))
HUB = 53
FROM_HUB = sorted((q for q in range(NSLAB) if q != HUB),
                  key=lambda q: HOPS((q // 32 - 1) % 2, (q // 8 % 4 - 2) % 4, (q % 8 - 5) % 8))


def state(prim):
    r, v0, v1, v2, p = prim
    m0, m1, m2 = r * v0, r * v1, r * v2
    energy = 1.5 * p + 0.5 * (m0 * v0 + m1 * v1 + m2 * v2)
    return (r, m0, m1, m2, energy)


def sound(prim):
    return jnp.sqrt(GAMMA * (prim[4] / prim[0]))


def side(prim, w, c, d):
    moving, p = prim[1 + d], prim[4]
    flux = [w[1 + d], w[1] * moving, w[2] * moving, w[3] * moving, (w[4] + p) * moving]
    flux[1 + d] = flux[1 + d] + p
    return w, flux, jnp.abs(moving) + c


def face(left, right):
    (wl, fl, al), (wr, fr, ar) = left, right
    a = jnp.maximum(al, ar)
    return [(fl[k] + fr[k]) - a * (wr[k] - wl[k]) for k in range(5)]


def cell(prim, d):
    return side(prim, state(prim), sound(prim), d)


def iota(shape, dim):
    return lax.broadcasted_iota(jnp.int32, shape, dim)


def comm_kernel(den, vel, pre, own_hbm, w_out, d_out, r_out, table, U, hs, hr, cm, cr, ms, mr, cs, xs, oh, ohc, base, ps, own, in_sem, hs_sem,
                hr_sem, xs_sem, xr_sem, loc_sem, as_sem, ar_sem, go):
    me = lax.axis_index("slab")
    sect = lax.axis_index("sect")
    far, row_y, row_z = me // 32, lax.rem(me // 8, 4), lax.rem(me, 8)
    owned = pltpu.make_async_copy(own_hbm, own, in_sem.at[6])
    copies = []
    for half in range(2):
        some, to = pl.ds(4 * half, 4), (pl.ds(1 + 4 * half, 4), pl.ds(8, CY))
        copies += [
            pltpu.make_async_copy(den.at[some], U.at[(0,) + to], in_sem.at[3 * half]),
            pltpu.make_async_copy(vel.at[:, some], U.at[(pl.ds(1, 3),) + to], in_sem.at[3 * half + 1]),
            pltpu.make_async_copy(pre.at[some], U.at[(4,) + to], in_sem.at[3 * half + 2]),
        ]
    for c in copies:
        c.start()
    owned.start()

    def slab_of(step_x, step_y, z):
        return lax.rem(far + step_x, 2) * 32 + lax.rem(row_y + step_y, 4) * 8 + z

    barrier = pltpu.get_barrier_semaphore()
    for i in range(1, NSECT):
        pl.semaphore_signal(barrier, inc=1, device_id={"sect": lax.rem(sect + i, NSECT)}, device_id_type=MESH)

    def tell(sem, q):
        pl.semaphore_signal(sem, inc=1, device_id={"slab": q}, device_id_type=MESH)

    after, before = lax.rem(me + 1, NSLAB), lax.rem(me + NSLAB - 1, NSLAB)

    @pl.when(me != HUB)
    def _():
        tell(barrier, HUB)

    @pl.when(after != HUB)
    def _():
        tell(barrier, after)

    @pl.when(before != HUB)
    def _():
        tell(barrier, before)

    best = jnp.zeros((8, 128), F32)
    for half in range(2):
        for c in copies[3 * half:3 * half + 3]:
            c.wait()
        for x in range(4 * half, 4 * half + 4):
            for yb in range(4):
                prim = [U[f, x + 1, 8 + 8 * yb:16 + 8 * yb, :] for f in range(5)]
                top = jnp.maximum(jnp.maximum(jnp.abs(prim[1]), jnp.abs(prim[2])), jnp.abs(prim[3])) + sound(prim)
                best = jnp.maximum(best, top)
    best = jnp.broadcast_to(jnp.max(best, keepdims=True), (8, 128))
    l8, s8 = iota((8, 128), 1), iota((8, 128), 0)
    pick = lax.rem(l8, 32) == s8 + 8
    for f in range(5):
        for way, y in ((0, 39), (1, 8)):
            edge = U[f, 1:9, y, :]
            hs[way, f] = edge
            turned = pltpu.roll(edge, 8, 1, stride=1, stride_axis=0)
            cm[way, f:f + 1, :] = jnp.sum(jnp.where(pick, turned, 0.0), axis=0, keepdims=True)
    for way in range(2):
        cm[way, 5:8, :] = best[5:8, :]
    ms[...] = best

    @pl.when(me != HUB)
    def _():
        pl.semaphore_wait(barrier, NSECT + 1)

    @pl.when(me == HUB)
    def _():
        pl.semaphore_wait(barrier, NSLAB - 1 + NSECT - 1)


    def remote(src, dst, ssem, rsem, where):
        return pltpu.make_async_remote_copy(src_ref=src, dst_ref=dst, send_sem=ssem, recv_sem=rsem, device_id=where,
                                            device_id_type=MESH)

    sects = [{"sect": lax.rem(sect + i, NSECT)} for i in range(NSECT)]
    near = [
        remote(cm.at[0], cr.at[0], hs_sem.at[0], hr_sem.at[0], sects[1]),
        remote(cm.at[1], cr.at[1], hs_sem.at[1], hr_sem.at[1], sects[3]),
        remote(ms, mr, hs_sem.at[2], hr_sem.at[2], sects[2]),
    ]
    sides = [
        remote(hs.at[0], hr.at[0], hs_sem.at[3], hr_sem.at[3], sects[1]),
        remote(hs.at[1], hr.at[1], hs_sem.at[4], hr_sem.at[4], sects[3]),
    ]
    ends = [
        remote(U.at[:, 8, pl.ds(8, CY)], U.at[:, 0, pl.ds(8, CY)], xs_sem.at[0], xr_sem.at[0], {"slab": after}),
        remote(U.at[:, 1, pl.ds(8, CY)], U.at[:, 9, pl.ds(8, CY)], xs_sem.at[1], xr_sem.at[1], {"slab": before}),
    ]
    for c in near + sides + ends:
        c.start()

    @pl.when(me == HUB)
    def _():
        for q in FROM_HUB:
            tell(go, q)

    owned.wait()
    row = jnp.concatenate([own[k].astype(F32) for k in range(4)], axis=1)
    across = jnp.broadcast_to(row, (128, 128))
    down = jnp.transpose(across)
    lane, sub = iota((128, 128), 1), iota((128, 128), 0)
    count = lambda i: lax.rem(i, 32) * 4 + i // 32
    earlier = jnp.where((across == down) & (count(sub) < count(lane)), 1.0, 0.0)
    rank = jnp.sum(earlier, axis=0, keepdims=True)
    target = row * MOST + rank
    slots = iota((NSLAB * MOST, 128), 0).astype(F32)
    oh[...] = jnp.where(slots == target, 1.0, 0.0).astype(jnp.bfloat16)
    target8, edges = jnp.broadcast_to(target, (8, 128)), jnp.full((8, 128), -1.0, F32)
    for part in range(3):
        for k in range(4):
            for e in range(2):
                to, source = 32 * part + 8 * k + e, 32 * k + 31 * e
                shift = (to - source) % 128
                edges = jnp.where(l8 == to, pltpu.roll(target8, shift, 1) if shift else target8, edges)
    ohc[...] = jnp.where(slots == edges[0:1, :], 1.0, 0.0).astype(jnp.bfloat16)

    wide = iota((CY, 128), 1)
    wide32 = lax.rem(wide, 32)
    for f in range(5):
        packed = jnp.ones((CY, 128), F32)
        for x in range(NXL):
            tile = U[f, x + 1, 8:40, :]
            for step in (-1, 0, 1):
                n = x + 8 * (step + 1)
                shift = (n - step) % 128
                packed = jnp.where(wide32 == n, pltpu.roll(tile, shift, 1) if shift else tile, packed)
        cs[f, 8:40, :] = packed
        cs[f, 7:8, :] = jnp.ones((1, 128), F32)
        cs[f, 40:41, :] = jnp.ones((1, 128), F32)

    middle = (lax.rem(l8, 32) >= 8) & (lax.rem(l8, 32) < 16)

    def gather_fields(items):
        total = None
        for j, item in items:
            shift = (8 * j - 8) % 128
            item = jnp.where(middle, item, 0.0)
            part = pltpu.roll(item, shift, 1) if shift else item
            total = part if total is None else total + part
        return total

    def of_line(groups, k):
        block = jnp.zeros((8, 128), F32)
        for g, group in groups.items():
            shift = (32 * g - 32 * k) % 128
            block = jnp.where(l8 // 32 == g, pltpu.roll(group, shift, 1) if shift else group, block)
        return block

    for yb in range(4):
        here = [cs[f, 8 + 8 * yb:16 + 8 * yb, :] for f in range(5)]
        above = [cs[f, 9 + 8 * yb:17 + 8 * yb, :] for f in range(5)]
        below = [cs[f, 7 + 8 * yb:15 + 8 * yb, :] for f in range(5)]
        w, c = state(here), sound(here)
        fz = face(side(here, w, c, 2), cell([pltpu.roll(a, 120, 1) for a in here], 2))
        centre = side(here, w, c, 1)
        fu, fd = face(centre, cell(above, 1)), face(cell(below, 1), centre)
        if yb == 0:
            fd = [jnp.where(s8 == 0, 0.0, a) for a in fd]
        if yb == 3:
            fu = [jnp.where(s8 == 7, 0.0, a) for a in fu]
        moved = [(fu[k] - fd[k]) + (fz[k] - pltpu.roll(fz[k], 8, 1)) for k in range(5)]
        items = list(here) + moved
        groups = {g: gather_fields(list(enumerate(items[4 * g:4 * g + 4]))) for g in range(3)}
        for k in range(4):
            xs[32 * k + 8 * yb:32 * k + 8 * yb + 8, :] = of_line(groups, k)

    def parts(a):
        hi = a.astype(jnp.bfloat16)
        rest = a - hi.astype(F32)
        mid = rest.astype(jnp.bfloat16)
        return hi, mid, (rest - mid.astype(F32)).astype(jnp.bfloat16)

    dot = functools.partial(jnp.dot, preferred_element_type=F32)
    hi, mid, lo = parts(xs[...])
    chosen = oh[...]
    base[...] = dot(chosen, hi) + (dot(chosen, mid) + dot(chosen, lo))

    for u in range(65):
        o = s8 + (8 * u - 8) - 8 * (l8 // 4)
        o = jnp.where(o >= NX // 2, o - NX, o)
        table[8 * u:8 * u + 8, :] = o.astype(F32)

    for c in near:
        c.wait_recv()
    first = s8 == 0
    left, right = [], []
    for f in range(5):
        wide8 = lambda a: jnp.broadcast_to(a, (8, 128))
        left.append(jnp.where(first, wide8(cr[0, f:f + 1, :]), wide8(cs[f, 39:40, :])))
        right.append(jnp.where(first, wide8(cs[f, 8:9, :]), wide8(cr[1, f:f + 1, :])))
    fe = [jnp.where(first, -a, a) for a in face(cell(left, 1), cell(right, 1))]
    groups = {1: gather_fields(list(enumerate(fe[:3], 1))), 2: gather_fields(list(enumerate(fe[3:])))}
    extra = parts(jnp.concatenate([of_line(groups, k) for k in range(4)], axis=0))
    blank = jnp.zeros((32, 128), jnp.bfloat16)
    added = dot(ohc[...], jnp.concatenate(list(extra) + [blank], axis=0))
    best = jnp.maximum(jnp.maximum(best, mr[...])[5:6, :], jnp.maximum(cr[0, 5:6, :], cr[1, 5:6, :]))
    sent = jnp.where(iota((NSLAB * MOST, 128), 1) >= 80, jnp.broadcast_to(best, (NSLAB * MOST, 128)), base[...] + added)
    ps[...] = sent.reshape(NSLAB, MOST, 128)

    def deliver(q):
        remote(ps.at[q], r_out.at[me], as_sem, ar_sem, {"slab": q}).start()

    @pl.when(me != HUB)
    def _():
        pl.semaphore_wait(go, 1)

    for a, b, c in PARTNERS:
        deliver(slab_of(a, b, lax.rem(row_z + c, 8)))
    mine = pltpu.make_async_copy(ps.at[me], r_out.at[me], loc_sem)
    mine.start()

    for c in sides:
        c.wait_recv()
    for f in range(5):
        U[f, 1:9, 7, :] = hr[0, f]
        U[f, 1:9, 40, :] = hr[1, f]

    def dense(x, carry):
        for yb in range(4):
            lo, hi = 8 + 8 * yb, 16 + 8 * yb
            here = [U[f, x + 1, lo:hi, :] for f in range(5)]
            w, c = state(here), sound(here)
            fz = face(side(here, w, c, 2), cell([pltpu.roll(a, 127, 1) for a in here], 2))
            moved = [fz[k] - pltpu.roll(fz[k], 1, 1) for k in range(5)]
            for d, pair in ((1, ((1, 1), (1, -1))), (0, ((2, 0), (0, 0)))):
                (xu, yu), (xd, yd) = pair
                mid = side(here, w, c, d)
                fu = face(mid, cell([U[f, x + xu, lo + yu:hi + yu, :] for f in range(5)], d))
                fd = face(cell([U[f, x + xd, lo + yd:hi + yd, :] for f in range(5)], d), mid)
                moved = [moved[k] + (fu[k] - fd[k]) for k in range(5)]
            for k in range(5):
                w_out[k, x, lo - 8:hi - 8, :] = w[k]
                d_out[k, x, lo - 8:hi - 8, :] = moved[k]
        return carry

    lax.fori_loop(1, NXL - 1, dense, 0)
    for c in ends:
        c.wait_recv()
    lax.fori_loop(0, 2, lambda i, carry: dense((NXL - 1) * i, carry), 0)

    mine.wait()
    for c in near + sides + ends:
        c.wait_send()
    most = pl.ds(0, NSLAB - 1)
    pltpu.make_async_copy(ps.at[most], ps.at[most], as_sem).wait()
    pltpu.make_async_copy(r_out.at[most], r_out.at[most], ar_sem).wait()


def final_kernel(w_ref, d_ref, r_ref, table, own_hbm, new_hbm, od, nb, pb, acc, own, sem, own_sem):
    me = lax.axis_index("slab").astype(F32)
    owned = pltpu.make_async_copy(own_hbm, own, own_sem)
    owned.start()
    arrived = r_ref[...]
    fastest = jnp.max(jnp.max(arrived, axis=0), axis=0, keepdims=True)[:, 96:97]
    half_dt = (0.5 * COURANT) / fastest
    hdt = jnp.broadcast_to(half_dt, (8, 128))

    outs = []
    for k in range(5):
        for x in range(NXL):
            for yb in range(4):
                at = (k, x, slice(8 * yb, 8 * yb + 8))
                nb[at] = w_ref[at] - hdt * d_ref[at]
        outs.append(pltpu.make_async_copy(nb.at[k], new_hbm.at[k], sem.at[k]))
        outs[-1].start()

    turned = jnp.transpose(arrived.reshape(NSLAB * MOST, 128))
    fields = [turned[8 * f:8 * f + 8, :] for f in range(10)]
    here, moved = fields[:5], fields[5:]
    s2 = iota((8, NSLAB * MOST), 0)

    def after(a):
        a = pltpu.roll(a, 7, 0)
        return jnp.where(s2 < 7, a, pltpu.roll(a, NSLAB * MOST - 4, 1))

    def before(a):
        a = pltpu.roll(a, 1, 0)
        return jnp.where(s2 > 0, a, pltpu.roll(a, 4, 1))

    w = state(here)
    fx = face(side(here, w, sound(here), 0), cell([after(a) for a in here], 0))
    hdt2 = jnp.broadcast_to(half_dt, (8, NSLAB * MOST))
    new = [w[k] - hdt2 * (moved[k] + (fx[k] - before(fx[k]))) for k in range(5)]
    r = new[0]
    v = [new[1 + k] / r for k in range(3)]
    p = (GAMMA - 1.0) * (new[4] - 0.5 * (new[1] * v[0] + new[2] * v[1] + new[3] * v[2]))
    broad = TURBULENT + p / r
    inverse = math.sqrt(LOG2E) / (8.0 * jnp.sqrt(broad))
    moved_by = (64.0 * v[0]) * inverse
    level = jnp.log2((NORMALISE / 8.0) * (r * r)) - 1.2 * jnp.log2(broad)
    for n, param in enumerate((inverse, moved_by, level)):
        for h in range(2):
            for x in range(8):
                pb[n, 8 * h + x] = jnp.broadcast_to(param[x:x + 1, 128 * h:128 * h + 128], (8, 128))

    def pixels(block, carry):
        first = pl.multiple_of(128 * block, 128)
        starts = (first, pl.multiple_of(lax.rem(first + NX // 2, NX), 128))
        sums = [None] * 16
        for h in range(2):
            for x in range(8):
                inv, mov, lev = (pb[n, 8 * h + x] for n in range(3))
                for j in range(16):
                    o = table[pl.ds(starts[h] + (8 * j + 8 - x), 8), :]
                    z = o * inv - mov
                    part = jnp.exp2(lev - z * z)
                    sums[j] = part if sums[j] is None else sums[j] + part
        for j in range(16):
            acc[pl.ds(first + 8 * j, 8), :] = sums[j]
        return carry

    lax.fori_loop(0, 4, pixels, 0)
    depth = jnp.transpose(acc[...])
    both = depth[0:8, :]
    for n in range(1, 16):
        both = both + depth[8 * n:8 * n + 8, :]
    owned.wait()
    row = jnp.concatenate([own[k].astype(F32) for k in range(4)], axis=1)
    held = jnp.sum(jnp.where(row == me, 1.0, 0.0), axis=1, keepdims=True)
    valid = iota((4, NX), 0).astype(F32) < held
    od[0, 0] = jnp.where(valid, both[0:4, :] + both[4:8, :], 0.0)
    for out in outs:
        out.wait()


def body(density, velocity, pressure, owners):
    own = jnp.transpose(owners, (1, 2, 0))
    density, velocity, pressure, own = (pltpu.with_memory_space_constraint(a, pltpu.HBM) for a in (density, velocity, pressure, own))
    vmem = pl.BlockSpec(memory_space=pltpu.VMEM)
    hbm = pl.BlockSpec(memory_space=pltpu.HBM)
    dense = jax.ShapeDtypeStruct((5, NXL, CY, NZ), F32)
    arrived = jax.ShapeDtypeStruct((NSLAB, MOST, 128), F32)
    offsets = jax.ShapeDtypeStruct((NX + 8, 128), F32)
    dma, regular = pltpu.SemaphoreType.DMA, pltpu.SemaphoreType.REGULAR
    w, d, r, table = pl.pallas_call(
        comm_kernel,
        out_shape=(dense, dense, arrived, offsets),
        in_specs=[hbm, hbm, hbm, hbm],
        out_specs=(vmem, vmem, vmem, vmem),
        scratch_shapes=[
            pltpu.VMEM((5, NXL + 2, CY + 16, NZ), F32),
            pltpu.VMEM((2, 5, 8, 128), F32),
            pltpu.VMEM((2, 5, 8, 128), F32),
            pltpu.VMEM((2, 8, 128), F32),
            pltpu.VMEM((2, 8, 128), F32),
            pltpu.VMEM((8, 128), F32),
            pltpu.VMEM((8, 128), F32),
            pltpu.VMEM((5, CY + 16, 128), F32),
            pltpu.VMEM((128, 128), F32),
            pltpu.VMEM((NSLAB * MOST, 128), jnp.bfloat16),
            pltpu.VMEM((NSLAB * MOST, 128), jnp.bfloat16),
            pltpu.VMEM((NSLAB * MOST, 128), F32),
            pltpu.VMEM((NSLAB, MOST, 128), F32),
            pltpu.VMEM((4, 1, CY), jnp.int32),
            dma((7,)), dma((5,)), dma((5,)), dma((2,)), dma((2,)), dma, dma, dma, regular,
        ],
        compiler_params=pltpu.CompilerParams(collective_id=0, has_side_effects=True, vmem_limit_bytes=24 << 20),
        name="exchange",
    )(density, velocity, pressure, own)
    return tuple(pl.pallas_call(
        final_kernel,
        out_shape=(dense, jax.ShapeDtypeStruct((1, 1, MOST, NX), F32)),
        in_specs=[vmem, vmem, vmem, vmem, hbm],
        out_specs=(hbm, vmem),
        scratch_shapes=[
            pltpu.VMEM((5, NXL, CY, NZ), F32),
            pltpu.VMEM((3, 16, 8, 128), F32),
            pltpu.VMEM((NX, 128), F32),
            pltpu.VMEM((4, 1, CY), jnp.int32),
            dma((5,)), dma,
        ],
        compiler_params=pltpu.CompilerParams(vmem_limit_bytes=24 << 20),
        name="finish",
    )(w, d, r, table, own))


def solution(mesh):
    placed = (P("slab", "sect", None), P(None, "slab", "sect", None), P("slab", "sect", None), P("sect", None, None))
    return jax.shard_map(body, mesh=mesh, in_specs=placed, out_specs=(P(None, "slab", "sect", None), P("sect", "slab", None, None)),
                         check_vma=False)
```

```python
import functools
import math

import jax
import jax.numpy as jnp
from jax import lax
from jax.experimental import pallas as pl
from jax.experimental.pallas import tpu as pltpu
from jax.sharding import PartitionSpec as P

MESH = pl.DeviceIdType.MESH
GAMMA = 5.0 / 3.0
COURANT = 0.15
TURBULENT = 0.25
NORMALISE = 0.5641895835477563
NSLAB = 64
NSECT = 4
NXL = 8
CY = 32
NZ = 128
MOST = 4
NX = 512
F32 = jnp.float32
LOG2E = math.log2(math.e)
HOPS = lambda a, b, c: 2 * a + min(b, 4 - b) + min(c, 8 - c)
FROM_ORIGIN = sorted(range(NSLAB), key=lambda q: HOPS(q // 32, q // 8 % 4, min(q % 8, 4)))
HUB = 53
FROM_HUB = sorted((q for q in range(NSLAB) if q != HUB),
                  key=lambda q: HOPS((q // 32 - 1) % 2, (q // 8 % 4 - 2) % 4, (q % 8 - 5) % 8))


def state(prim):
    r, v0, v1, v2, p = prim
    m0, m1, m2 = r * v0, r * v1, r * v2
    energy = 1.5 * p + 0.5 * (m0 * v0 + m1 * v1 + m2 * v2)
    return (r, m0, m1, m2, energy)


def sound(prim):
    return jnp.sqrt(GAMMA * (prim[4] / prim[0]))


def side(prim, w, c, d):
    moving, p = prim[1 + d], prim[4]
    flux = [w[1 + d], w[1] * moving, w[2] * moving, w[3] * moving, (w[4] + p) * moving]
    flux[1 + d] = flux[1 + d] + p
    return w, flux, jnp.abs(moving) + c


def face(left, right):
    (wl, fl, al), (wr, fr, ar) = left, right
    a = jnp.maximum(al, ar)
    return [(fl[k] + fr[k]) - a * (wr[k] - wl[k]) for k in range(5)]


def cell(prim, d):
    return side(prim, state(prim), sound(prim), d)


def iota(shape, dim):
    return lax.broadcasted_iota(jnp.int32, shape, dim)


def comm_kernel(den, vel, pre, own_hbm, w_out, d_out, r_out, table, U, hs, hr, cm, cr, ms, mr, cs, xs, oh, ohc, base, ps, own, in_sem, hs_sem,
                hr_sem, xs_sem, xr_sem, loc_sem, as_sem, ar_sem, go):
    me = lax.axis_index("slab")
    sect = lax.axis_index("sect")
    owned = pltpu.make_async_copy(own_hbm, own, in_sem.at[6])
    copies = []
    for half in range(2):
        some, to = pl.ds(4 * half, 4), (pl.ds(1 + 4 * half, 4), pl.ds(8, CY))
        copies += [
            pltpu.make_async_copy(den.at[some], U.at[(0,) + to], in_sem.at[3 * half]),
            pltpu.make_async_copy(vel.at[:, some], U.at[(pl.ds(1, 3),) + to], in_sem.at[3 * half + 1]),
            pltpu.make_async_copy(pre.at[some], U.at[(4,) + to], in_sem.at[3 * half + 2]),
        ]
    barrier = pltpu.get_barrier_semaphore()
    for i in range(1, NSECT):
        pl.semaphore_signal(barrier, inc=1, device_id={"sect": lax.rem(sect + i, NSECT)}, device_id_type=MESH)

    for c in copies:
        c.start()
    owned.start()

    def tell(sem, q):
        pl.semaphore_signal(sem, inc=1, device_id={"slab": q}, device_id_type=MESH)

    after, before = lax.rem(me + 1, NSLAB), lax.rem(me + NSLAB - 1, NSLAB)

    @pl.when(me != HUB)
    def _():
        tell(barrier, HUB)

    @pl.when(after != HUB)
    def _():
        tell(barrier, after)

    @pl.when(before != HUB)
    def _():
        tell(barrier, before)

    best = jnp.zeros((8, 128), F32)
    for half in range(2):
        for c in copies[3 * half:3 * half + 3]:
            c.wait()
        for x in range(4 * half, 4 * half + 4):
            for yb in range(4):
                prim = [U[f, x + 1, 8 + 8 * yb:16 + 8 * yb, :] for f in range(5)]
                top = jnp.maximum(jnp.maximum(jnp.abs(prim[1]), jnp.abs(prim[2])), jnp.abs(prim[3])) + sound(prim)
                best = jnp.maximum(best, top)
    best = jnp.broadcast_to(jnp.max(best, keepdims=True), (8, 128))
    l8, s8 = iota((8, 128), 1), iota((8, 128), 0)
    pick = lax.rem(l8, 32) == s8 + 8
    for f in range(5):
        for way, y in ((0, 39), (1, 8)):
            edge = U[f, 1:9, y, :]
            hs[way, f] = edge
            turned = pltpu.roll(edge, 8, 1, stride=1, stride_axis=0)
            cm[way, f:f + 1, :] = jnp.sum(jnp.where(pick, turned, 0.0), axis=0, keepdims=True)
    for way in range(2):
        cm[way, 5:6, :] = best[5:6, :]
        cm[way, 6:7, :] = sound([cm[way, f:f + 1, :] for f in range(5)])
        cm[way, 7:8, :] = best[7:8, :]
    ms[...] = best

    @pl.when(me != HUB)
    def _():
        pl.semaphore_wait(barrier, NSECT + 1)

    @pl.when(me == HUB)
    def _():
        pl.semaphore_wait(barrier, NSLAB - 1 + NSECT - 1)


    def remote(src, dst, ssem, rsem, where):
        return pltpu.make_async_remote_copy(src_ref=src, dst_ref=dst, send_sem=ssem, recv_sem=rsem, device_id=where,
                                            device_id_type=MESH)

    sects = [{"sect": lax.rem(sect + i, NSECT)} for i in range(NSECT)]
    near = [
        remote(cm.at[0], cr.at[0], hs_sem.at[0], hr_sem.at[0], sects[1]),
        remote(cm.at[1], cr.at[1], hs_sem.at[1], hr_sem.at[1], sects[3]),
        remote(ms, mr, hs_sem.at[2], hr_sem.at[2], sects[2]),
    ]
    sides = [
        remote(hs.at[0], hr.at[0], hs_sem.at[3], hr_sem.at[3], sects[1]),
        remote(hs.at[1], hr.at[1], hs_sem.at[4], hr_sem.at[4], sects[3]),
    ]
    ends = [
        remote(U.at[:, 8, pl.ds(8, CY)], U.at[:, 0, pl.ds(8, CY)], xs_sem.at[0], xr_sem.at[0], {"slab": after}),
        remote(U.at[:, 1, pl.ds(8, CY)], U.at[:, 9, pl.ds(8, CY)], xs_sem.at[1], xr_sem.at[1], {"slab": before}),
    ]
    for c in near + sides + ends:
        c.start()

    @pl.when(me == HUB)
    def _():
        for q in FROM_HUB:
            tell(go, q)

    owned.wait()
    row = jnp.concatenate([own[k].astype(F32) for k in range(4)], axis=1)
    across = jnp.broadcast_to(row, (128, 128))
    down = jnp.transpose(across)
    lane, sub = iota((128, 128), 1), iota((128, 128), 0)
    count = lambda i: lax.rem(i, 32) * 4 + i // 32
    earlier = jnp.where((across == down) & (count(sub) < count(lane)), 1.0, 0.0)
    rank = jnp.sum(earlier, axis=0, keepdims=True)
    target = row * MOST + rank
    slots = iota((NSLAB * MOST, 128), 0).astype(F32)
    oh[...] = jnp.where(slots == target, 1.0, 0.0).astype(jnp.bfloat16)
    target8, edges = jnp.broadcast_to(target, (8, 128)), jnp.full((8, 128), -1.0, F32)
    for part in range(3):
        for k in range(4):
            for e in range(2):
                to, source = 32 * part + 8 * k + e, 32 * k + 31 * e
                shift = (to - source) % 128
                edges = jnp.where(l8 == to, pltpu.roll(target8, shift, 1) if shift else target8, edges)
    ohc[...] = jnp.where(slots == edges[0:1, :], 1.0, 0.0).astype(jnp.bfloat16)

    wide = iota((CY, 128), 1)
    wide32 = lax.rem(wide, 32)
    for f in range(5):
        packed = jnp.ones((CY, 128), F32)
        for x in range(NXL):
            tile = U[f, x + 1, 8:40, :]
            for step in (-1, 0, 1):
                n = x + 8 * (step + 1)
                shift = (n - step) % 128
                packed = jnp.where(wide32 == n, pltpu.roll(tile, shift, 1) if shift else tile, packed)
        cs[f, 8:40, :] = packed
        cs[f, 7:8, :] = jnp.ones((1, 128), F32)
        cs[f, 40:41, :] = jnp.ones((1, 128), F32)

    middle = (lax.rem(l8, 32) >= 8) & (lax.rem(l8, 32) < 16)

    def gather_fields(items):
        total = None
        for j, item in items:
            shift = (8 * j - 8) % 128
            item = jnp.where(middle, item, 0.0)
            part = pltpu.roll(item, shift, 1) if shift else item
            total = part if total is None else total + part
        return total

    def of_line(groups, k):
        block = jnp.zeros((8, 128), F32)
        for g, group in groups.items():
            shift = (32 * g - 32 * k) % 128
            block = jnp.where(l8 // 32 == g, pltpu.roll(group, shift, 1) if shift else group, block)
        return block

    for yb in range(4):
        here = [cs[f, 8 + 8 * yb:16 + 8 * yb, :] for f in range(5)]
        above = [cs[f, 9 + 8 * yb:17 + 8 * yb, :] for f in range(5)]
        below = [cs[f, 7 + 8 * yb:15 + 8 * yb, :] for f in range(5)]
        w, c = state(here), sound(here)
        fz = face(side(here, w, c, 2), cell([pltpu.roll(a, 120, 1) for a in here], 2))
        centre = side(here, w, c, 1)
        fu, fd = face(centre, cell(above, 1)), face(cell(below, 1), centre)
        if yb == 0:
            fd = [jnp.where(s8 == 0, 0.0, a) for a in fd]
        if yb == 3:
            fu = [jnp.where(s8 == 7, 0.0, a) for a in fu]
        moved = [(fu[k] - fd[k]) + (fz[k] - pltpu.roll(fz[k], 8, 1)) for k in range(5)]
        items = list(here) + moved
        groups = {g: gather_fields(list(enumerate(items[4 * g:4 * g + 4]))) for g in range(3)}
        for k in range(4):
            xs[32 * k + 8 * yb:32 * k + 8 * yb + 8, :] = of_line(groups, k)

    def parts(a):
        hi = a.astype(jnp.bfloat16)
        rest = a - hi.astype(F32)
        mid = rest.astype(jnp.bfloat16)
        return hi, mid, (rest - mid.astype(F32)).astype(jnp.bfloat16)

    dot = functools.partial(jnp.dot, preferred_element_type=F32)
    hi, mid, lo = parts(xs[...])
    chosen = oh[...]
    base[...] = dot(chosen, hi) + (dot(chosen, mid) + dot(chosen, lo))

    for u in range(65):
        o = s8 + (8 * u - 8) - 8 * (l8 // 4)
        o = jnp.where(o >= NX // 2, o - NX, o)
        table[8 * u:8 * u + 8, :] = o.astype(F32)

    first = s8 == 0
    sign = jnp.where(first, -1.0, 1.0)
    wide8 = lambda low, high: jnp.where(first, jnp.broadcast_to(low, (8, 128)), jnp.broadcast_to(high, (8, 128)))
    wk, fk, ak = cell([wide8(cs[f, 8:9, :], cs[f, 39:40, :]) for f in range(5)], 1)
    for c in near:
        c.wait_recv()
    beyond = [wide8(cr[0, f:f + 1, :], cr[1, f:f + 1, :]) for f in range(7)]
    wb, fb, ab = side(beyond[:5], state(beyond[:5]), beyond[6], 1)
    speed = jnp.maximum(ak, ab)
    fe = [jnp.where(middle, sign * (fk[k] + fb[k]) + speed * (wk[k] - wb[k]), 0.0) for k in range(5)]

    def edge_lines(k):
        total = None
        for f in range(5):
            shift = (8 * (5 + f) - 8 - 32 * k) % 128
            part = jnp.where(l8 // 8 == 5 + f, pltpu.roll(fe[f], shift, 1) if shift else fe[f], 0.0)
            total = part if total is None else total + part
        return total

    extra = parts(jnp.concatenate([edge_lines(k) for k in range(4)], axis=0))
    blank = jnp.zeros((32, 128), jnp.bfloat16)
    added = dot(ohc[...], jnp.concatenate(list(extra) + [blank], axis=0))
    best = jnp.maximum(jnp.maximum(best, mr[...])[5:6, :], jnp.maximum(cr[0, 5:6, :], cr[1, 5:6, :]))
    sent = jnp.where(iota((NSLAB * MOST, 128), 1) >= 80, jnp.broadcast_to(best, (NSLAB * MOST, 128)), base[...] + added)
    ps[...] = sent.reshape(NSLAB, MOST, 128)

    def deliver(q):
        remote(ps.at[q], r_out.at[me], as_sem, ar_sem, {"slab": q}).start()

    @pl.when(me != HUB)
    def _():
        pl.semaphore_wait(go, 1)

    for q in FROM_ORIGIN:
        pl.when(q != me)(functools.partial(deliver, q))
    mine = pltpu.make_async_copy(ps.at[me], r_out.at[me], loc_sem)
    mine.start()

    for c in sides:
        c.wait_recv()
    for f in range(5):
        U[f, 1:9, 7, :] = hr[0, f]
        U[f, 1:9, 40, :] = hr[1, f]

    def dense(x, carry):
        for yb in range(4):
            lo, hi = 8 + 8 * yb, 16 + 8 * yb
            here = [U[f, x + 1, lo:hi, :] for f in range(5)]
            w, c = state(here), sound(here)
            fz = face(side(here, w, c, 2), cell([pltpu.roll(a, 127, 1) for a in here], 2))
            moved = [fz[k] - pltpu.roll(fz[k], 1, 1) for k in range(5)]
            for d, pair in ((1, ((1, 1), (1, -1))), (0, ((2, 0), (0, 0)))):
                (xu, yu), (xd, yd) = pair
                mid = side(here, w, c, d)
                fu = face(mid, cell([U[f, x + xu, lo + yu:hi + yu, :] for f in range(5)], d))
                fd = face(cell([U[f, x + xd, lo + yd:hi + yd, :] for f in range(5)], d), mid)
                moved = [moved[k] + (fu[k] - fd[k]) for k in range(5)]
            for k in range(5):
                w_out[k, x, lo - 8:hi - 8, :] = w[k]
                d_out[k, x, lo - 8:hi - 8, :] = moved[k]
        return carry

    lax.fori_loop(1, NXL - 1, dense, 0)
    for c in ends:
        c.wait_recv()
    lax.fori_loop(0, 2, lambda i, carry: dense((NXL - 1) * i, carry), 0)

    mine.wait()
    for c in near + sides + ends:
        c.wait_send()
    most = pl.ds(0, NSLAB - 1)
    pltpu.make_async_copy(ps.at[most], ps.at[most], as_sem).wait()
    pltpu.make_async_copy(r_out.at[most], r_out.at[most], ar_sem).wait()


def final_kernel(w_ref, d_ref, r_ref, table, own_hbm, new_hbm, od, nb, pb, acc, own, sem, own_sem):
    me = lax.axis_index("slab").astype(F32)
    owned = pltpu.make_async_copy(own_hbm, own, own_sem)
    owned.start()
    arrived = r_ref[...]
    fastest = jnp.max(jnp.max(arrived, axis=0), axis=0, keepdims=True)[:, 96:97]
    half_dt = (0.5 * COURANT) / fastest
    hdt = jnp.broadcast_to(half_dt, (8, 128))

    outs = []
    for k in range(5):
        for x in range(NXL):
            for yb in range(4):
                at = (k, x, slice(8 * yb, 8 * yb + 8))
                nb[at] = w_ref[at] - hdt * d_ref[at]
        outs.append(pltpu.make_async_copy(nb.at[k], new_hbm.at[k], sem.at[k]))
        outs[-1].start()

    turned = jnp.transpose(arrived.reshape(NSLAB * MOST, 128))
    fields = [turned[8 * f:8 * f + 8, :] for f in range(10)]
    here, moved = fields[:5], fields[5:]
    s2 = iota((8, NSLAB * MOST), 0)

    def after(a):
        a = pltpu.roll(a, 7, 0)
        return jnp.where(s2 < 7, a, pltpu.roll(a, NSLAB * MOST - 4, 1))

    def before(a):
        a = pltpu.roll(a, 1, 0)
        return jnp.where(s2 > 0, a, pltpu.roll(a, 4, 1))

    w = state(here)
    fx = face(side(here, w, sound(here), 0), cell([after(a) for a in here], 0))
    hdt2 = jnp.broadcast_to(half_dt, (8, NSLAB * MOST))
    new = [w[k] - hdt2 * (moved[k] + (fx[k] - before(fx[k]))) for k in range(5)]
    r = new[0]
    v = [new[1 + k] / r for k in range(3)]
    p = (GAMMA - 1.0) * (new[4] - 0.5 * (new[1] * v[0] + new[2] * v[1] + new[3] * v[2]))
    broad = TURBULENT + p / r
    inverse = math.sqrt(LOG2E) / (8.0 * jnp.sqrt(broad))
    moved_by = (64.0 * v[0]) * inverse
    level = jnp.log2((NORMALISE / 8.0) * (r * r)) - 1.2 * jnp.log2(broad)
    for n, param in enumerate((inverse, moved_by, level)):
        for h in range(2):
            for x in range(8):
                pb[n, 8 * h + x] = jnp.broadcast_to(param[x:x + 1, 128 * h:128 * h + 128], (8, 128))

    def pixels(block, carry):
        first = pl.multiple_of(128 * block, 128)
        starts = (first, pl.multiple_of(lax.rem(first + NX // 2, NX), 128))
        sums = [None] * 16
        for h in range(2):
            for x in range(8):
                inv, mov, lev = (pb[n, 8 * h + x] for n in range(3))
                for j in range(16):
                    o = table[pl.ds(starts[h] + (8 * j + 8 - x), 8), :]
                    z = o * inv - mov
                    part = jnp.exp2(lev - z * z)
                    sums[j] = part if sums[j] is None else sums[j] + part
        for j in range(16):
            acc[pl.ds(first + 8 * j, 8), :] = sums[j]
        return carry

    lax.fori_loop(0, 4, pixels, 0)
    depth = jnp.transpose(acc[...])
    both = depth[0:8, :]
    for n in range(1, 16):
        both = both + depth[8 * n:8 * n + 8, :]
    owned.wait()
    row = jnp.concatenate([own[k].astype(F32) for k in range(4)], axis=1)
    held = jnp.sum(jnp.where(row == me, 1.0, 0.0), axis=1, keepdims=True)
    valid = iota((4, NX), 0).astype(F32) < held
    od[0, 0] = jnp.where(valid, both[0:4, :] + both[4:8, :], 0.0)
    for out in outs:
        out.wait()


def body(density, velocity, pressure, owners):
    own = jnp.transpose(owners, (1, 2, 0))
    density, velocity, pressure, own = (pltpu.with_memory_space_constraint(a, pltpu.HBM) for a in (density, velocity, pressure, own))
    vmem = pl.BlockSpec(memory_space=pltpu.VMEM)
    hbm = pl.BlockSpec(memory_space=pltpu.HBM)
    dense = jax.ShapeDtypeStruct((5, NXL, CY, NZ), F32)
    arrived = jax.ShapeDtypeStruct((NSLAB, MOST, 128), F32)
    offsets = jax.ShapeDtypeStruct((NX + 8, 128), F32)
    dma, regular = pltpu.SemaphoreType.DMA, pltpu.SemaphoreType.REGULAR
    w, d, r, table = pl.pallas_call(
        comm_kernel,
        out_shape=(dense, dense, arrived, offsets),
        in_specs=[hbm, hbm, hbm, hbm],
        out_specs=(vmem, vmem, vmem, vmem),
        scratch_shapes=[
            pltpu.VMEM((5, NXL + 2, CY + 16, NZ), F32),
            pltpu.VMEM((2, 5, 8, 128), F32),
            pltpu.VMEM((2, 5, 8, 128), F32),
            pltpu.VMEM((2, 8, 128), F32),
            pltpu.VMEM((2, 8, 128), F32),
            pltpu.VMEM((8, 128), F32),
            pltpu.VMEM((8, 128), F32),
            pltpu.VMEM((5, CY + 16, 128), F32),
            pltpu.VMEM((128, 128), F32),
            pltpu.VMEM((NSLAB * MOST, 128), jnp.bfloat16),
            pltpu.VMEM((NSLAB * MOST, 128), jnp.bfloat16),
            pltpu.VMEM((NSLAB * MOST, 128), F32),
            pltpu.VMEM((NSLAB, MOST, 128), F32),
            pltpu.VMEM((4, 1, CY), jnp.int32),
            dma((7,)), dma((5,)), dma((5,)), dma((2,)), dma((2,)), dma, dma, dma, regular,
        ],
        compiler_params=pltpu.CompilerParams(collective_id=0, has_side_effects=True, vmem_limit_bytes=24 << 20),
        name="exchange",
    )(density, velocity, pressure, own)
    return tuple(pl.pallas_call(
        final_kernel,
        out_shape=(dense, jax.ShapeDtypeStruct((1, 1, MOST, NX), F32)),
        in_specs=[vmem, vmem, vmem, vmem, hbm],
        out_specs=(hbm, vmem),
        scratch_shapes=[
            pltpu.VMEM((5, NXL, CY, NZ), F32),
            pltpu.VMEM((3, 16, 8, 128), F32),
            pltpu.VMEM((NX, 128), F32),
            pltpu.VMEM((4, 1, CY), jnp.int32),
            dma((5,)), dma,
        ],
        compiler_params=pltpu.CompilerParams(vmem_limit_bytes=24 << 20),
        name="finish",
    )(w, d, r, table, own))


def solution(mesh):
    placed = (P("slab", "sect", None), P(None, "slab", "sect", None), P("slab", "sect", None), P("sect", None, None))
    return jax.shard_map(body, mesh=mesh, in_specs=placed, out_specs=(P(None, "slab", "sect", None), P("sect", "slab", None, None)),
                         check_vma=False)
```

```python
import functools
import math

import jax
import jax.numpy as jnp
from jax import lax
from jax.experimental import pallas as pl
from jax.experimental.pallas import tpu as pltpu
from jax.sharding import PartitionSpec as P

MESH = pl.DeviceIdType.MESH
GAMMA = 5.0 / 3.0
COURANT = 0.15
TURBULENT = 0.25
NORMALISE = 0.5641895835477563
NSLAB = 64
NSECT = 4
NXL = 8
CY = 32
NZ = 128
MOST = 4
NX = 512
F32 = jnp.float32
LOG2E = math.log2(math.e)
HOPS = lambda a, b, c: 2 * a + min(b, 4 - b) + min(c, 8 - c)
FROM_ORIGIN = sorted(range(NSLAB), key=lambda q: HOPS(q // 32, q // 8 % 4, min(q % 8, 4)))
HUB = 53
FROM_HUB = sorted((q for q in range(NSLAB) if q != HUB),
                  key=lambda q: HOPS((q // 32 - 1) % 2, (q // 8 % 4 - 2) % 4, (q % 8 - 5) % 8))


def state(prim):
    r, v0, v1, v2, p = prim
    m0, m1, m2 = r * v0, r * v1, r * v2
    energy = 1.5 * p + 0.5 * (m0 * v0 + m1 * v1 + m2 * v2)
    return (r, m0, m1, m2, energy)


def sound(prim):
    return jnp.sqrt(GAMMA * (prim[4] / prim[0]))


def side(prim, w, c, d):
    moving, p = prim[1 + d], prim[4]
    flux = [w[1 + d], w[1] * moving, w[2] * moving, w[3] * moving, (w[4] + p) * moving]
    flux[1 + d] = flux[1 + d] + p
    return w, flux, jnp.abs(moving) + c


def face(left, right):
    (wl, fl, al), (wr, fr, ar) = left, right
    a = jnp.maximum(al, ar)
    return [(fl[k] + fr[k]) - a * (wr[k] - wl[k]) for k in range(5)]


def cell(prim, d):
    return side(prim, state(prim), sound(prim), d)


def iota(shape, dim):
    return lax.broadcasted_iota(jnp.int32, shape, dim)


def comm_kernel(den, vel, pre, own_hbm, w_out, d_out, r_out, table, U, hs, hr, cm, cr, ms, mr, cs, xs, oh, ohc, base, ps, own, in_sem, hs_sem,
                hr_sem, xs_sem, xr_sem, loc_sem, as_sem, ar_sem, go):
    me = lax.axis_index("slab")
    sect = lax.axis_index("sect")
    owned = pltpu.make_async_copy(own_hbm, own, in_sem.at[6])
    copies = []
    for half in range(2):
        some, to = pl.ds(4 * half, 4), (pl.ds(1 + 4 * half, 4), pl.ds(8, CY))
        copies += [
            pltpu.make_async_copy(den.at[some], U.at[(0,) + to], in_sem.at[3 * half]),
            pltpu.make_async_copy(vel.at[:, some], U.at[(pl.ds(1, 3),) + to], in_sem.at[3 * half + 1]),
            pltpu.make_async_copy(pre.at[some], U.at[(4,) + to], in_sem.at[3 * half + 2]),
        ]
    barrier = pltpu.get_barrier_semaphore()
    for i in range(1, NSECT):
        pl.semaphore_signal(barrier, inc=1, device_id={"sect": lax.rem(sect + i, NSECT)}, device_id_type=MESH)

    for c in copies:
        c.start()
    owned.start()

    def tell(sem, q):
        pl.semaphore_signal(sem, inc=1, device_id={"slab": q}, device_id_type=MESH)

    after, before = lax.rem(me + 1, NSLAB), lax.rem(me + NSLAB - 1, NSLAB)

    @pl.when(me != HUB)
    def _():
        tell(barrier, HUB)

    @pl.when(after != HUB)
    def _():
        tell(barrier, after)

    @pl.when(before != HUB)
    def _():
        tell(barrier, before)

    best = jnp.zeros((8, 128), F32)
    for half in range(2):
        for c in copies[3 * half:3 * half + 3]:
            c.wait()
        for x in range(4 * half, 4 * half + 4):
            for yb in range(4):
                prim = [U[f, x + 1, 8 + 8 * yb:16 + 8 * yb, :] for f in range(5)]
                top = jnp.maximum(jnp.maximum(jnp.abs(prim[1]), jnp.abs(prim[2])), jnp.abs(prim[3])) + sound(prim)
                best = jnp.maximum(best, top)
    best = jnp.broadcast_to(jnp.max(best, keepdims=True), (8, 128))
    l8, s8 = iota((8, 128), 1), iota((8, 128), 0)
    pick = lax.rem(l8, 32) == s8 + 8
    for f in range(5):
        for way, y in ((0, 39), (1, 8)):
            edge = U[f, 1:9, y, :]
            hs[way, f] = edge
            turned = pltpu.roll(edge, 8, 1, stride=1, stride_axis=0)
            cm[way, f:f + 1, :] = jnp.sum(jnp.where(pick, turned, 0.0), axis=0, keepdims=True)
    for way in range(2):
        cm[way, 5:6, :] = best[5:6, :]
        cm[way, 6:7, :] = sound([cm[way, f:f + 1, :] for f in range(5)])
        cm[way, 7:8, :] = best[7:8, :]
    ms[...] = best

    @pl.when(me != HUB)
    def _():
        pl.semaphore_wait(barrier, NSECT + 1)

    @pl.when(me == HUB)
    def _():
        pl.semaphore_wait(barrier, NSLAB - 1 + NSECT - 1)


    def remote(src, dst, ssem, rsem, where):
        return pltpu.make_async_remote_copy(src_ref=src, dst_ref=dst, send_sem=ssem, recv_sem=rsem, device_id=where,
                                            device_id_type=MESH)

    sects = [{"sect": lax.rem(sect + i, NSECT)} for i in range(NSECT)]
    near = [
        remote(cm.at[0], cr.at[0], hs_sem.at[0], hr_sem.at[0], sects[1]),
        remote(cm.at[1], cr.at[1], hs_sem.at[1], hr_sem.at[1], sects[3]),
        remote(ms, mr, hs_sem.at[2], hr_sem.at[2], sects[2]),
    ]
    sides = [
        remote(hs.at[0], hr.at[0], hs_sem.at[3], hr_sem.at[3], sects[1]),
        remote(hs.at[1], hr.at[1], hs_sem.at[4], hr_sem.at[4], sects[3]),
    ]
    ends = [
        remote(U.at[:, 8, pl.ds(8, CY)], U.at[:, 0, pl.ds(8, CY)], xs_sem.at[0], xr_sem.at[0], {"slab": after}),
        remote(U.at[:, 1, pl.ds(8, CY)], U.at[:, 9, pl.ds(8, CY)], xs_sem.at[1], xr_sem.at[1], {"slab": before}),
    ]
    for c in near + sides + ends:
        c.start()

    @pl.when(me == HUB)
    def _():
        for q in FROM_HUB:
            tell(go, q)

    owned.wait()
    row = jnp.concatenate([own[k].astype(F32) for k in range(4)], axis=1)
    across = jnp.broadcast_to(row, (128, 128))
    down = jnp.transpose(across)
    lane, sub = iota((128, 128), 1), iota((128, 128), 0)
    count = lambda i: lax.rem(i, 32) * 4 + i // 32
    earlier = jnp.where((across == down) & (count(sub) < count(lane)), 1.0, 0.0)
    rank = jnp.sum(earlier, axis=0, keepdims=True)
    target = row * MOST + rank
    slots = iota((NSLAB * MOST, 128), 0).astype(F32)
    oh[...] = jnp.where(slots == target, 1.0, 0.0).astype(jnp.bfloat16)
    target8, edges = jnp.broadcast_to(target, (8, 128)), jnp.full((8, 128), -1.0, F32)
    for part in range(3):
        for k in range(4):
            for e in range(2):
                to, source = 32 * part + 8 * k + e, 32 * k + 31 * e
                shift = (to - source) % 128
                edges = jnp.where(l8 == to, pltpu.roll(target8, shift, 1) if shift else target8, edges)
    ohc[...] = jnp.where(slots == edges[0:1, :], 1.0, 0.0).astype(jnp.bfloat16)

    wide = iota((CY, 128), 1)
    wide32 = lax.rem(wide, 32)
    for f in range(5):
        packed = jnp.ones((CY, 128), F32)
        for x in range(NXL):
            tile = U[f, x + 1, 8:40, :]
            for step in (-1, 0, 1):
                n = x + 8 * (step + 1)
                shift = (n - step) % 128
                packed = jnp.where(wide32 == n, pltpu.roll(tile, shift, 1) if shift else tile, packed)
        cs[f, 8:40, :] = packed
        cs[f, 7:8, :] = jnp.ones((1, 128), F32)
        cs[f, 40:41, :] = jnp.ones((1, 128), F32)

    middle = (lax.rem(l8, 32) >= 8) & (lax.rem(l8, 32) < 16)

    def gather_fields(items):
        total = None
        for j, item in items:
            shift = (8 * j - 8) % 128
            item = jnp.where(middle, item, 0.0)
            part = pltpu.roll(item, shift, 1) if shift else item
            total = part if total is None else total + part
        return total

    def of_line(groups, k):
        block = jnp.zeros((8, 128), F32)
        for g, group in groups.items():
            shift = (32 * g - 32 * k) % 128
            block = jnp.where(l8 // 32 == g, pltpu.roll(group, shift, 1) if shift else group, block)
        return block

    for yb in range(4):
        here = [cs[f, 8 + 8 * yb:16 + 8 * yb, :] for f in range(5)]
        above = [cs[f, 9 + 8 * yb:17 + 8 * yb, :] for f in range(5)]
        below = [cs[f, 7 + 8 * yb:15 + 8 * yb, :] for f in range(5)]
        w, c = state(here), sound(here)
        fz = face(side(here, w, c, 2), cell([pltpu.roll(a, 120, 1) for a in here], 2))
        centre = side(here, w, c, 1)
        fu, fd = face(centre, cell(above, 1)), face(cell(below, 1), centre)
        if yb == 0:
            fd = [jnp.where(s8 == 0, 0.0, a) for a in fd]
        if yb == 3:
            fu = [jnp.where(s8 == 7, 0.0, a) for a in fu]
        moved = [(fu[k] - fd[k]) + (fz[k] - pltpu.roll(fz[k], 8, 1)) for k in range(5)]
        items = list(here) + moved
        groups = {g: gather_fields(list(enumerate(items[4 * g:4 * g + 4]))) for g in range(3)}
        for k in range(4):
            xs[32 * k + 8 * yb:32 * k + 8 * yb + 8, :] = of_line(groups, k)

    def parts(a):
        hi = a.astype(jnp.bfloat16)
        rest = a - hi.astype(F32)
        mid = rest.astype(jnp.bfloat16)
        return hi, mid, (rest - mid.astype(F32)).astype(jnp.bfloat16)

    dot = functools.partial(jnp.dot, preferred_element_type=F32)
    hi, mid, lo = parts(xs[...])
    chosen = oh[...]
    base[...] = dot(chosen, hi) + (dot(chosen, mid) + dot(chosen, lo))

    for u in range(65):
        o = s8 + (8 * u - 8) - 8 * (l8 // 4)
        o = jnp.where(o >= NX // 2, o - NX, o)
        table[8 * u:8 * u + 8, :] = o.astype(F32)

    first = s8 == 0
    sign = jnp.where(first, -1.0, 1.0)
    wide8 = lambda low, high: jnp.where(first, jnp.broadcast_to(low, (8, 128)), jnp.broadcast_to(high, (8, 128)))
    wk, fk, ak = cell([wide8(cs[f, 8:9, :], cs[f, 39:40, :]) for f in range(5)], 1)
    for c in near:
        c.wait_recv()
    beyond = [wide8(cr[0, f:f + 1, :], cr[1, f:f + 1, :]) for f in range(7)]
    wb, fb, ab = side(beyond[:5], state(beyond[:5]), beyond[6], 1)
    speed = jnp.maximum(ak, ab)
    fe = [jnp.where(middle, sign * (fk[k] + fb[k]) + speed * (wk[k] - wb[k]), 0.0) for k in range(5)]

    def edge_lines(k):
        total = None
        for f in range(5):
            shift = (8 * (5 + f) - 8 - 32 * k) % 128
            part = jnp.where(l8 // 8 == 5 + f, pltpu.roll(fe[f], shift, 1) if shift else fe[f], 0.0)
            total = part if total is None else total + part
        return total

    extra = parts(jnp.concatenate([edge_lines(k) for k in range(4)], axis=0))
    blank = jnp.zeros((32, 128), jnp.bfloat16)
    added = dot(ohc[...], jnp.concatenate(list(extra) + [blank], axis=0))
    best = jnp.maximum(jnp.maximum(best, mr[...])[5:6, :], jnp.maximum(cr[0, 5:6, :], cr[1, 5:6, :]))
    sent = jnp.where(iota((NSLAB * MOST, 128), 1) >= 80, jnp.broadcast_to(best, (NSLAB * MOST, 128)), base[...] + added)
    ps[...] = sent.reshape(NSLAB, MOST, 128)

    def deliver(q):
        remote(ps.at[q], r_out.at[me], as_sem, ar_sem, {"slab": q}).start()

    @pl.when(me != HUB)
    def _():
        pl.semaphore_wait(go, 1)

    for q in FROM_ORIGIN:
        pl.when(q != me)(functools.partial(deliver, q))
    mine = pltpu.make_async_copy(ps.at[me], r_out.at[me], loc_sem)
    mine.start()

    for c in sides:
        c.wait_recv()
    for f in range(5):
        U[f, 1:9, 7, :] = hr[0, f]
        U[f, 1:9, 40, :] = hr[1, f]

    def dense(x, carry):
        for yb in range(4):
            lo, hi = 8 + 8 * yb, 16 + 8 * yb
            here = [U[f, x + 1, lo:hi, :] for f in range(5)]
            w, c = state(here), sound(here)
            fz = face(side(here, w, c, 2), cell([pltpu.roll(a, 127, 1) for a in here], 2))
            moved = [fz[k] - pltpu.roll(fz[k], 1, 1) for k in range(5)]
            for d, pair in ((1, ((1, 1), (1, -1))), (0, ((2, 0), (0, 0)))):
                (xu, yu), (xd, yd) = pair
                mid = side(here, w, c, d)
                fu = face(mid, cell([U[f, x + xu, lo + yu:hi + yu, :] for f in range(5)], d))
                fd = face(cell([U[f, x + xd, lo + yd:hi + yd, :] for f in range(5)], d), mid)
                moved = [moved[k] + (fu[k] - fd[k]) for k in range(5)]
            for k in range(5):
                w_out[k, x, lo - 8:hi - 8, :] = w[k]
                d_out[k, x, lo - 8:hi - 8, :] = moved[k]
        return carry

    lax.fori_loop(1, NXL - 1, dense, 0)
    for c in ends:
        c.wait_recv()
    lax.fori_loop(0, 2, lambda i, carry: dense((NXL - 1) * i, carry), 0)

    mine.wait()
    for c in near + sides + ends:
        c.wait_send()
    most = pl.ds(0, NSLAB - 1)
    pltpu.make_async_copy(ps.at[most], ps.at[most], as_sem).wait()
    pltpu.make_async_copy(r_out.at[most], r_out.at[most], ar_sem).wait()


def final_kernel(w_ref, d_ref, r_ref, table, own_hbm, new_hbm, od, nb, pb, acc, own, sem, own_sem):
    me = lax.axis_index("slab").astype(F32)
    owned = pltpu.make_async_copy(own_hbm, own, own_sem)
    owned.start()
    arrived = r_ref[...]
    fastest = jnp.max(jnp.max(arrived, axis=0), axis=0, keepdims=True)[:, 96:97]
    half_dt = (0.5 * COURANT) / fastest
    hdt = jnp.broadcast_to(half_dt, (8, 128))

    outs = []
    for k in range(5):
        for x in range(NXL):
            for yb in range(4):
                at = (k, x, slice(8 * yb, 8 * yb + 8))
                nb[at] = w_ref[at] - hdt * d_ref[at]
        outs.append(pltpu.make_async_copy(nb.at[k], new_hbm.at[k], sem.at[k]))
        outs[-1].start()

    turned = jnp.transpose(arrived.reshape(NSLAB * MOST, 128))
    fields = [turned[8 * f:8 * f + 8, :] for f in range(10)]
    here, moved = fields[:5], fields[5:]
    s2 = iota((8, NSLAB * MOST), 0)

    def after(a):
        a = pltpu.roll(a, 7, 0)
        return jnp.where(s2 < 7, a, pltpu.roll(a, NSLAB * MOST - 4, 1))

    def before(a):
        a = pltpu.roll(a, 1, 0)
        return jnp.where(s2 > 0, a, pltpu.roll(a, 4, 1))

    w = state(here)
    fx = face(side(here, w, sound(here), 0), cell([after(a) for a in here], 0))
    hdt2 = jnp.broadcast_to(half_dt, (8, NSLAB * MOST))
    new = [w[k] - hdt2 * (moved[k] + (fx[k] - before(fx[k]))) for k in range(5)]
    r = new[0]
    v = [new[1 + k] / r for k in range(3)]
    p = (GAMMA - 1.0) * (new[4] - 0.5 * (new[1] * v[0] + new[2] * v[1] + new[3] * v[2]))
    broad = TURBULENT + p / r
    inverse = math.sqrt(LOG2E) / (8.0 * jnp.sqrt(broad))
    moved_by = (64.0 * v[0]) * inverse
    level = jnp.log2((NORMALISE / 8.0) * (r * r)) - 1.2 * jnp.log2(broad)
    for n, param in enumerate((inverse, moved_by, level)):
        for h in range(2):
            for x in range(8):
                pb[n, 8 * h + x] = jnp.broadcast_to(param[x:x + 1, 128 * h:128 * h + 128], (8, 128))

    def pixels(block, carry):
        first = pl.multiple_of(256 * block, 256)
        starts = (first, pl.multiple_of(lax.rem(first + NX // 2, NX), 256))
        sums = [None] * 32
        for h in range(2):
            for x in range(8):
                inv, mov, lev = (pb[n, 8 * h + x] for n in range(3))
                for j in range(32):
                    o = table[pl.ds(starts[h] + (8 * j + 8 - x), 8), :]
                    z = o * inv - mov
                    part = jnp.exp2(lev - z * z)
                    sums[j] = part if sums[j] is None else sums[j] + part
        for j in range(32):
            acc[pl.ds(first + 8 * j, 8), :] = sums[j]
        return carry

    lax.fori_loop(0, 2, pixels, 0)
    depth = jnp.transpose(acc[...])
    both = depth[0:8, :]
    for n in range(1, 16):
        both = both + depth[8 * n:8 * n + 8, :]
    owned.wait()
    row = jnp.concatenate([own[k].astype(F32) for k in range(4)], axis=1)
    held = jnp.sum(jnp.where(row == me, 1.0, 0.0), axis=1, keepdims=True)
    valid = iota((4, NX), 0).astype(F32) < held
    od[0, 0] = jnp.where(valid, both[0:4, :] + both[4:8, :], 0.0)
    for out in outs:
        out.wait()


def body(density, velocity, pressure, owners):
    own = jnp.transpose(owners, (1, 2, 0))
    density, velocity, pressure, own = (pltpu.with_memory_space_constraint(a, pltpu.HBM) for a in (density, velocity, pressure, own))
    vmem = pl.BlockSpec(memory_space=pltpu.VMEM)
    hbm = pl.BlockSpec(memory_space=pltpu.HBM)
    dense = jax.ShapeDtypeStruct((5, NXL, CY, NZ), F32)
    arrived = jax.ShapeDtypeStruct((NSLAB, MOST, 128), F32)
    offsets = jax.ShapeDtypeStruct((NX + 8, 128), F32)
    dma, regular = pltpu.SemaphoreType.DMA, pltpu.SemaphoreType.REGULAR
    w, d, r, table = pl.pallas_call(
        comm_kernel,
        out_shape=(dense, dense, arrived, offsets),
        in_specs=[hbm, hbm, hbm, hbm],
        out_specs=(vmem, vmem, vmem, vmem),
        scratch_shapes=[
            pltpu.VMEM((5, NXL + 2, CY + 16, NZ), F32),
            pltpu.VMEM((2, 5, 8, 128), F32),
            pltpu.VMEM((2, 5, 8, 128), F32),
            pltpu.VMEM((2, 8, 128), F32),
            pltpu.VMEM((2, 8, 128), F32),
            pltpu.VMEM((8, 128), F32),
            pltpu.VMEM((8, 128), F32),
            pltpu.VMEM((5, CY + 16, 128), F32),
            pltpu.VMEM((128, 128), F32),
            pltpu.VMEM((NSLAB * MOST, 128), jnp.bfloat16),
            pltpu.VMEM((NSLAB * MOST, 128), jnp.bfloat16),
            pltpu.VMEM((NSLAB * MOST, 128), F32),
            pltpu.VMEM((NSLAB, MOST, 128), F32),
            pltpu.VMEM((4, 1, CY), jnp.int32),
            dma((7,)), dma((5,)), dma((5,)), dma((2,)), dma((2,)), dma, dma, dma, regular,
        ],
        compiler_params=pltpu.CompilerParams(collective_id=0, has_side_effects=True, vmem_limit_bytes=24 << 20),
        name="exchange",
    )(density, velocity, pressure, own)
    return tuple(pl.pallas_call(
        final_kernel,
        out_shape=(dense, jax.ShapeDtypeStruct((1, 1, MOST, NX), F32)),
        in_specs=[vmem, vmem, vmem, vmem, hbm],
        out_specs=(hbm, vmem),
        scratch_shapes=[
            pltpu.VMEM((5, NXL, CY, NZ), F32),
            pltpu.VMEM((3, 16, 8, 128), F32),
            pltpu.VMEM((NX, 128), F32),
            pltpu.VMEM((4, 1, CY), jnp.int32),
            dma((5,)), dma,
        ],
        compiler_params=pltpu.CompilerParams(vmem_limit_bytes=24 << 20),
        name="finish",
    )(w, d, r, table, own))


def solution(mesh):
    placed = (P("slab", "sect", None), P(None, "slab", "sect", None), P("slab", "sect", None), P("sect", None, None))
    return jax.shard_map(body, mesh=mesh, in_specs=placed, out_specs=(P(None, "slab", "sect", None), P("sect", "slab", None, None)),
                         check_vma=False)
```
